32 devices in a mesh: stn: 8 (over z, x), tf: 4 (over y, core).
Axes of the slice: x: 2, y: 2, z: 4, core: 2. Of those that a mesh axis runs over, the one named last changes fastest.
Arguments:
- voltages: bfloat16 [2, 64, 2, 131072], P(None, 'stn', None, 'tf'), may hold values from -6 to 6
- delay_table: float32 [128, 64], replicated, may hold values from -512 to 512
- beam_pointing: int32 [32], replicated, may hold values from 0 to 127
- station_group: int32 [64], replicated, may hold values from 0 to 3
Outputs:
- beams: bfloat16 [32, 2, 2, 32, 32, 128], P('stn', None, None, None, 'tf')
The draws below stay inside these ranges and needn't reach their ends.
All inputs are finite; a program needn't handle non-finite values.
Results may differ from the reference program's by a relative error of at most 0.0082.
Values may be sent and summed in bfloat16 or wider, within the bound.
No kernel may reach another device: no remote copies, remote signals or barrier semaphores. Data moves between devices by JAX's collectives and lax.ppermute only.
A program may use at most 128 MiB of HBM per device.

```python
import math
import jax
import jax.numpy as jnp
from jax import lax

TAPS = 16
CH_LO = 32
CH_HI = 128
BEAMS = 32
GROUPS = 4
DIRS = 128
STATIONS = 64
FRAMES = 32
SAMPLES = 131072


def place_ends(array, stream_key, smallest, largest):
    place = [jax.random.randint(jax.random.fold_in(stream_key, axis), (), 0, length) for axis, length in enumerate(array.shape)]
    longest = array.shape.index(max(array.shape))
    neighbour = place[:longest] + [(place[longest] + 1) % array.shape[longest]] + place[longest + 1:]
    return array.at[tuple(place)].set(smallest).at[tuple(neighbour)].set(largest)


def levels(stream_key, extent, shards, low, top_value):
    level, own = 1.0, jax.random.fold_in(stream_key, 6)
    for axis_at, blocks in shards:
        heights = jnp.exp(jax.random.uniform(jax.random.fold_in(own, axis_at), (blocks,), jnp.float32, low / len(shards), top_value / len(shards)))
        level = level * jnp.repeat(heights, extent[axis_at] // blocks).reshape([-1 if axis == axis_at else 1 for axis in range(len(extent))])
    return level


def centred(rng, dims, width, reach, pieces=(), kind=jnp.bfloat16):
    drawn = width * jax.random.normal(rng, dims, jnp.float32)
    if pieces:
        drawn = drawn * levels(rng, dims, pieces, -0.22, 0.18)
    return jnp.clip(drawn, -reach, reach).astype(kind)


def setup_inputs(seed: int = 0) -> dict:
    key_of = jax.random.split(jax.random.key(seed), 5)
    return {
        "voltages": centred(key_of[0], (2, STATIONS, 2, SAMPLES), 1.0, 6.0, ((1, 8), (3, 4))),
        "delay_table": jnp.clip(jax.random.uniform(key_of[1], (DIRS, STATIONS), jnp.float32, -512.0, 512.0), -512.0, 512.0),
        "beam_pointing": place_ends(jax.random.randint(key_of[2], (BEAMS,), 0, DIRS), jax.random.fold_in(key_of[2], 1), 0, DIRS - 1).astype(jnp.int32),
        "station_group": place_ends(jax.random.randint(key_of[3], (STATIONS,), 0, GROUPS), jax.random.fold_in(key_of[3], 1), 0, GROUPS - 1).astype(jnp.int32),
    }


TWO_PI = 2.0 * math.pi

def filter_window(tap_count, points):
    position = jnp.arange(tap_count * points, dtype=jnp.int32).astype(jnp.float32)
    total_len = float(tap_count * points)
    hann_taper = 0.5 - 0.5 * jnp.cos(TWO_PI / total_len * position)
    kernel = jnp.sinc((position - 0.5 * total_len) / float(points)) * hann_taper
    return kernel.reshape(tap_count, points)

def dft_table(points):
    counter = jnp.arange(points, dtype=jnp.int32)
    product = counter[:, None] * counter[None, :] % points
    angles = TWO_PI / points * product.astype(jnp.float32)
    factor = 1.0 / math.sqrt(points)
    cosine = jnp.cos(angles) * factor
    sine_part = jnp.sin(angles) * factor
    stacked = jnp.stack([jnp.stack([cosine, sine_part]), jnp.stack([-sine_part, cosine])])
    return stacked.astype(jnp.bfloat16)

def channelize(extended, frame_count):
    points = CH_LO * CH_HI
    window = filter_window(TAPS, points)
    filtered = sum((window[tap_step] * extended[:, :, :, tap_step:tap_step + frame_count, :].astype(jnp.float32) for tap_step in range(TAPS)))
    filtered = filtered.astype(jnp.bfloat16)
    shaped = filtered.reshape(filtered.shape[:4] + (CH_LO, CH_HI))
    section_one = jnp.einsum('oikn,ispfnm->ospfkm', dft_table(CH_LO).astype(jnp.float32), shaped.astype(jnp.float32))
    low_index = jnp.arange(CH_LO, dtype=jnp.int32)
    high_index = jnp.arange(CH_HI, dtype=jnp.int32)
    twiddle = TWO_PI / points * (low_index[:, None] * high_index[None, :]).astype(jnp.float32)
    cosine = jnp.cos(twiddle)
    sine_part = jnp.sin(twiddle)
    rotated = jnp.stack([section_one[0] * cosine + section_one[1] * sine_part, section_one[1] * cosine - section_one[0] * sine_part]).astype(jnp.bfloat16)
    return jnp.einsum('oimj,ispfkm->ospfkj', dft_table(CH_HI).astype(jnp.float32), rotated.astype(jnp.float32)).astype(jnp.bfloat16)

def beam_weights(delays, beam_ids, groups, channel_low, station_total):
    points = CH_LO * CH_HI
    member = (groups[None, :] == (beam_ids % GROUPS)[:, None]).astype(jnp.float32)
    weight_scale = math.sqrt(GROUPS / station_total) * member
    channel = channel_low[:, None] + CH_LO * jnp.arange(CH_HI, dtype=jnp.int32)[None, :]
    fraction = channel.astype(jnp.float32) / float(points)
    phases = TWO_PI * (delays[:, :, None, None] * fraction[None, None])
    weight_re = (weight_scale[:, :, None, None] * jnp.cos(phases)).astype(jnp.bfloat16)
    weight_im = (-weight_scale[:, :, None, None] * jnp.sin(phases)).astype(jnp.bfloat16)
    return (weight_re, weight_im)

def form_beams(weight_re, weight_im, channels):
    real_in = channels[0]
    imag_in = channels[1]

    def contract(weights_part, data_part):
        return jnp.einsum('bsxc,spfxc->bpfxc', weights_part.astype(jnp.float32), data_part.astype(jnp.float32))
    real_out = contract(weight_re, real_in) - contract(weight_im, imag_in)
    imag_out = contract(weight_re, imag_in) + contract(weight_im, real_in)
    return jnp.stack([real_out, imag_out], axis=1)

def reference(voltages, delay_table, beam_pointing, station_group):
    points = CH_LO * CH_HI

    def one_station(samples):
        framed = samples.reshape(2, 1, 2, FRAMES, points)
        padded = jnp.concatenate([jnp.zeros((2, 1, 2, TAPS - 1, points), samples.dtype), framed], axis=3)
        return channelize(padded, FRAMES)[:, 0]
    per_station = lax.map(one_station, jnp.moveaxis(voltages, 1, 0))
    delays = delay_table[beam_pointing]
    beam_ids = jnp.arange(BEAMS, dtype=jnp.int32)

    def one_low(low_pick):
        sliced = lax.dynamic_index_in_dim(per_station, low_pick, 4, keepdims=True)
        sliced = jnp.moveaxis(sliced, 1, 0)
        channel_low = jnp.reshape(low_pick, (1,)).astype(jnp.int32)
        weight_re, weight_im = beam_weights(delays, beam_ids, station_group, channel_low, STATIONS)
        return form_beams(weight_re, weight_im, sliced)[:, :, :, :, 0, :].astype(jnp.bfloat16)
    stacked = lax.map(one_low, jnp.arange(CH_LO, dtype=jnp.int32))
    return jnp.moveaxis(stacked, 0, 4)
```

```python
import functools
import math

import jax
import jax.numpy as jnp
from jax import lax
from jax.experimental import pallas as pl
from jax.experimental.pallas import tpu as pltpu
from jax.sharding import PartitionSpec as P

TAPS = 16
CH_LO = 32
CH_HI = 128
GROUPS = 4
POINTS = CH_LO * CH_HI
TWO_PI = 2.0 * math.pi
BF = jnp.bfloat16
F32 = jnp.float32

LANES = 128
TF = 4
STN = 8
PART = CH_HI // TF
LOW = CH_LO // TF
PER = 4


def filter_window(position):
    total_len = float(TAPS * POINTS)
    value = position.astype(F32)
    hann_taper = 0.5 - 0.5 * jnp.cos(TWO_PI / total_len * value)
    return jnp.sinc((value - 0.5 * total_len) / float(POINTS)) * hann_taper


def window_rows(part):
    shape = (TAPS, 2 * CH_LO, LANES)
    tap = lax.broadcasted_iota(jnp.int32, shape, 0)
    n2 = lax.broadcasted_iota(jnp.int32, shape, 1) // 2
    n1 = part * PART + lax.broadcasted_iota(jnp.int32, shape, 2) % PART
    return filter_window(tap * POINTS + n2 * CH_HI + n1)


def dft_pair(points):
    counter = jnp.arange(points, dtype=jnp.int32)
    product = counter[:, None] * counter[None, :] % points
    angles = TWO_PI / points * product.astype(F32)
    factor = 1.0 / math.sqrt(points)
    return jnp.cos(angles) * factor, jnp.sin(angles) * factor


def first_table():
    cosine, sine = dft_pair(CH_LO)
    planes = jnp.stack([jnp.stack([cosine, sine]), jnp.stack([-sine, cosine])])
    planes = planes.reshape(2, 2, TF, LOW, CH_LO)
    both = jnp.eye(2, dtype=F32)
    table = jnp.einsum("oitkn,pr->otpkinr", planes, both)
    return table.reshape(4 * CH_LO, 4 * CH_LO).astype(BF)


def second_table():
    cosine, sine = dft_pair(CH_HI)
    table = jnp.concatenate(
        [jnp.concatenate([cosine, -sine], axis=1), jnp.concatenate([sine, cosine], axis=1)], axis=0
    )
    return table.astype(BF)


def twiddle_rows(part):
    shape = (2 * CH_LO, LANES)
    row = lax.broadcasted_iota(jnp.int32, shape, 0)
    k2 = row // (2 * LOW) * LOW + row % LOW
    n1 = part * PART + lax.broadcasted_iota(jnp.int32, shape, 1) % PART
    angle = TWO_PI / POINTS * (k2 * n1).astype(F32)
    return jnp.cos(angle), jnp.sin(angle)


def swap_lane_blocks(parts):
    return [
        jnp.concatenate([part[:, j * PART : (j + 1) * PART] for part in parts], axis=1)
        for j in range(len(parts))
    ]


def spread_kernel(volt_ref, out_ref):
    parts = [volt_ref[0, a] for a in range(PER)]
    for j, block in enumerate(swap_lane_blocks(parts)):
        out_ref[j, 0, 0] = block


def spread(volt):
    planes, stations, rows, _ = volt.shape
    groups = stations // PER
    return pl.pallas_call(
        spread_kernel,
        name="spread",
        grid=(planes, groups),
        in_specs=[pl.BlockSpec((1, PER, rows, LANES), lambda q, c: (q, c, 0, 0))],
        out_specs=pl.BlockSpec((TF, 1, 1, rows, LANES), lambda q, c: (0, q, c, 0, 0)),
        out_shape=jax.ShapeDtypeStruct((TF, planes, groups, rows, LANES), BF),
    )(volt)


def channel_kernel(frames, blocks_ref, win_ref, table_ref, cos_ref, sin_ref, out_ref, wide_ref, filt_ref):
    sources = blocks_ref.shape[0]
    per_source = frames // sources
    rows = 2 * CH_LO
    history = TAPS - 1
    wide_ref[:, 0:history] = jnp.zeros((2, history, rows, LANES), F32)
    for q in range(2):
        for src in range(sources):
            block = blocks_ref[src, q, 0].astype(F32)
            wide_ref[q, pl.ds(history + src * per_source, per_source)] = block.reshape(
                per_source, rows, LANES
            )

    strip = 16

    def one_strip(step, carry):
        q = step // (rows // strip)
        at = pl.multiple_of(step % (rows // strip) * strip, strip)
        for f in range(frames):
            total = None
            for tap in range(max(0, history - f), TAPS):
                term = win_ref[tap, pl.ds(at, strip), :] * wide_ref[q, f + tap, pl.ds(at, strip), :]
                total = term if total is None else total + term
            filt_ref[f, q, pl.ds(at, strip), :] = total.astype(BF)
        return carry

    lax.fori_loop(0, 2 * rows // strip, one_strip, 0)

    table = table_ref[...]
    cosine, sine = cos_ref[...], sin_ref[...]
    per_dest = frames // STN

    def one_pair(pair, carry):
        left = filt_ref[2 * pair].reshape(2 * rows, LANES)
        right = filt_ref[2 * pair + 1].reshape(2 * rows, LANES)
        both = jnp.concatenate([left, right], axis=1)
        spectrum = jnp.dot(table, both, preferred_element_type=F32)
        for side in range(2):
            f = 2 * pair + side
            real = spectrum[:rows, side * LANES : (side + 1) * LANES]
            imag = spectrum[rows:, side * LANES : (side + 1) * LANES]
            turned = (real * cosine + imag * sine, imag * cosine - real * sine)
            for o in range(2):
                value = turned[o].astype(BF)
                out_ref[f // per_dest, :, o, 0, f % per_dest] = value.reshape(TF, 2 * LOW, LANES)
        return carry

    lax.fori_loop(0, frames // 2, one_pair, 0)


def channel_step(blocks, window, table, cosine, sine):
    sources, planes, groups, rows, _ = blocks.shape
    frames = sources * rows // (2 * CH_LO)
    per_dest = frames // STN
    whole = lambda shape: pl.BlockSpec(shape, lambda c: (0,) * len(shape))
    return pl.pallas_call(
        functools.partial(channel_kernel, frames),
        name="channel_step",
        grid=(groups,),
        in_specs=[
            pl.BlockSpec((sources, planes, 1, rows, LANES), lambda c: (0, 0, c, 0, 0)),
            whole(window.shape),
            whole(table.shape),
            whole(cosine.shape),
            whole(sine.shape),
        ],
        out_specs=pl.BlockSpec(
            (STN, TF, planes, 1, per_dest, 2 * LOW, LANES), lambda c: (0, 0, 0, c, 0, 0, 0)
        ),
        out_shape=jax.ShapeDtypeStruct((STN, TF, planes, groups, per_dest, 2 * LOW, LANES), BF),
        scratch_shapes=[
            pltpu.VMEM((planes, frames + TAPS - 1, 2 * CH_LO, LANES), F32),
            pltpu.VMEM((frames, planes, 2 * CH_LO, LANES), BF),
        ],
    )(blocks, window, table, cosine, sine)


def weight_kernel(low_ref, table_ref, beam_ref, group_ref, out_ref, order_ref, start_ref):
    stations = group_ref.shape[0]
    per_group = out_ref.shape[1]
    scale = math.sqrt(GROUPS / stations)
    shape = (LOW, LANES)
    k2 = low_ref[0] + lax.broadcasted_iota(jnp.int32, shape, 0)
    channel = k2 + CH_LO * lax.broadcasted_iota(jnp.int32, shape, 1)
    fraction = channel.astype(F32) / float(POINTS)

    def one_station(s, carry):
        group = group_ref[s]
        for i in range(per_group):
            turns = table_ref[beam_ref[group + GROUPS * i], s] * fraction
            quarter = jnp.round(4.0 * turns)
            angle = TWO_PI * (turns - 0.25 * quarter)
            square = angle * angle
            sine = angle * (
                1.0 + square * (-1.0 / 6 + square * (1.0 / 120 + square * (-1.0 / 5040 + square * (1.0 / 362880))))
            )
            cosine = 1.0 + square * (
                -0.5 + square * (1.0 / 24 + square * (-1.0 / 720 + square * (1.0 / 40320)))
            )
            turn = quarter.astype(jnp.int32) & 3
            odd = (turn & 1) == 1
            base_cos = jnp.where(odd, sine, cosine)
            base_sin = jnp.where(odd, cosine, sine)
            real = jnp.where((turn == 1) | (turn == 2), -base_cos, base_cos)
            imag = jnp.where(turn >= 2, -base_sin, base_sin)
            out_ref[s, i, 0] = (scale * real).astype(BF).astype(F32)
            out_ref[s, i, 1] = (-scale * imag).astype(BF).astype(F32)
        return carry

    lax.fori_loop(0, stations, one_station, 0)

    at = jnp.int32(0)
    for g in range(GROUPS):
        start_ref[g] = at

        def put(s, at, g=g):
            mine = group_ref[s] == g

            @pl.when(mine)
            def _():
                order_ref[at] = s

            return at + mine.astype(jnp.int32)

        at = lax.fori_loop(0, stations, put, at)
    start_ref[GROUPS] = at


def beam_weights(low, delay_table, beam_pointing, station_group):
    stations = station_group.shape[0]
    per_group = beam_pointing.shape[0] // GROUPS
    smem = pl.BlockSpec(memory_space=pltpu.SMEM)
    return pl.pallas_call(
        weight_kernel,
        name="beam_weights",
        in_specs=[smem] * 4,
        out_specs=[pl.BlockSpec(memory_space=pltpu.VMEM), smem, smem],
        out_shape=[
            jax.ShapeDtypeStruct((stations, per_group, 2, LOW, LANES), F32),
            jax.ShapeDtypeStruct((stations,), jnp.int32),
            jax.ShapeDtypeStruct((GROUPS + 1,), jnp.int32),
        ],
    )(low, delay_table, beam_pointing, station_group)


def beam_kernel(blocks_ref, table_ref, weight_ref, order_ref, start_ref, out_ref, chan_ref):
    src = pl.program_id(0)
    groups, per_dest = blocks_ref.shape[3], blocks_ref.shape[4]
    rows = per_dest * 2 * LOW
    table = table_ref[...]
    for c in range(groups):
        planes = []
        for o in range(2):
            parts = [blocks_ref[0, j, o, c].reshape(rows, LANES) for j in range(TF)]
            planes.append(swap_lane_blocks(parts))
        for a in range(PER):
            both = jnp.concatenate([planes[0][a], planes[1][a]], axis=1)
            spectrum = jnp.dot(both, table, preferred_element_type=F32)
            at = src * (groups * PER) + c * PER + a
            for o in range(2):
                chan_ref[at, o] = spectrum[:, o * LANES : (o + 1) * LANES].reshape(
                    per_dest * 2, LOW, LANES
                )

    @pl.when(src == pl.num_programs(0) - 1)
    def _():
        per_group = weight_ref.shape[1]

        def one_block(step, carry):
            g = step // per_dest
            f = step % per_dest

            def one_station(pos, acc):
                s = order_ref[pos]
                new = []
                data = [(chan_ref[s, 0, 2 * f + p], chan_ref[s, 1, 2 * f + p]) for p in range(2)]
                for i in range(per_group):
                    wre, wim = weight_ref[s, i, 0], weight_ref[s, i, 1]
                    for p in range(2):
                        re, im = data[p]
                        are, aim = acc[4 * i + 2 * p], acc[4 * i + 2 * p + 1]
                        new.append(are + (wre * re - wim * im))
                        new.append(aim + (wre * im + wim * re))
                return tuple(new)

            zero = jnp.zeros((LOW, LANES), F32)
            acc = lax.fori_loop(
                start_ref[g], start_ref[g + 1], one_station, (zero,) * (4 * per_group)
            )
            for i in range(per_group):
                for p in range(2):
                    for o in range(2):
                        out_ref[i, g, o, p, f] = acc[4 * i + 2 * p + o].astype(BF)
            return carry

        lax.fori_loop(0, GROUPS * per_dest, one_block, 0)


def beam_step(blocks, table, weights, order, start):
    sources, parts, planes, groups, per_dest, _, _ = blocks.shape
    stations, per_group = weights.shape[:2]
    smem = pl.BlockSpec(memory_space=pltpu.SMEM)
    out = (per_group, GROUPS, planes, 2, per_dest, LOW, LANES)
    return pl.pallas_call(
        beam_kernel,
        name="beam_step",
        grid=(sources,),
        in_specs=[
            pl.BlockSpec((1,) + blocks.shape[1:], lambda s: (s, 0, 0, 0, 0, 0, 0)),
            pl.BlockSpec(table.shape, lambda s: (0, 0)),
            pl.BlockSpec(memory_space=pltpu.VMEM),
            smem,
            smem,
        ],
        out_specs=pl.BlockSpec(out, lambda s: (0,) * len(out)),
        out_shape=jax.ShapeDtypeStruct(out, BF),
        scratch_shapes=[pltpu.VMEM((stations, planes, 2 * per_dest, LOW, LANES), F32)],
    )(blocks, table, weights, order, start)


def fast_body(voltages, delay_table, beam_pointing, station_group):
    planes, stations_here, pols, samples_here = voltages.shape
    part = lax.axis_index("tf")
    chunks = samples_here // LANES
    volt = voltages.reshape(planes, stations_here, pols, chunks, LANES)
    volt = volt.transpose(0, 1, 3, 2, 4).reshape(planes, stations_here, chunks * pols, LANES)

    blocks = spread(volt)
    blocks = lax.all_to_all(blocks, "tf", split_axis=0, concat_axis=0, tiled=True)
    cosine, sine = twiddle_rows(part)
    turned = channel_step(blocks, window_rows(part), first_table(), cosine, sine)

    shape = turned.shape
    turned = turned.reshape((STN * TF,) + shape[2:])
    turned = lax.all_to_all(turned, ("stn", "tf"), split_axis=0, concat_axis=0, tiled=True)
    turned = turned.reshape(shape)

    low = (part * LOW).astype(jnp.int32).reshape(1)
    weights, order, start = beam_weights(low, delay_table, beam_pointing, station_group)
    beams = beam_step(turned, second_table(), weights, order, start)
    beams = lax.all_to_all(beams, "stn", split_axis=0, concat_axis=0, tiled=True)
    beams = beams.transpose(1, 2, 3, 0, 4, 5, 6)
    return beams.reshape(beams.shape[:3] + (-1,) + beams.shape[5:])


def passed_along(value, axis, steps):
    count = lax.axis_size(axis)
    first, last = (max(0, -steps), min(count, count - steps))
    return lax.ppermute(value, axis, [(source, source + steps) for source in range(first, last)])


def plain_window(tap_count, points):
    position = jnp.arange(tap_count * points, dtype=jnp.int32).astype(jnp.float32)
    total_len = float(tap_count * points)
    hann_taper = 0.5 - 0.5 * jnp.cos(TWO_PI / total_len * position)
    kernel = jnp.sinc((position - 0.5 * total_len) / float(points)) * hann_taper
    return kernel.reshape(tap_count, points)


def dft_table(points):
    counter = jnp.arange(points, dtype=jnp.int32)
    product = counter[:, None] * counter[None, :] % points
    angles = TWO_PI / points * product.astype(jnp.float32)
    factor = 1.0 / math.sqrt(points)
    cosine = jnp.cos(angles) * factor
    sine_part = jnp.sin(angles) * factor
    stacked = jnp.stack([jnp.stack([cosine, sine_part]), jnp.stack([-sine_part, cosine])])
    return stacked.astype(jnp.bfloat16)


def channelize(extended, frame_count):
    points = CH_LO * CH_HI
    window = plain_window(TAPS, points)
    filtered = sum(
        (
            window[tap_step]
            * extended[:, :, :, tap_step : tap_step + frame_count, :].astype(jnp.float32)
            for tap_step in range(TAPS)
        )
    )
    filtered = filtered.astype(jnp.bfloat16)
    shaped = filtered.reshape(filtered.shape[:4] + (CH_LO, CH_HI))
    section_one = jnp.einsum(
        "oikn,ispfnm->ospfkm", dft_table(CH_LO), shaped, preferred_element_type=jnp.float32
    )
    low_index = jnp.arange(CH_LO, dtype=jnp.int32)
    high_index = jnp.arange(CH_HI, dtype=jnp.int32)
    twiddle = TWO_PI / points * (low_index[:, None] * high_index[None, :]).astype(jnp.float32)
    cosine = jnp.cos(twiddle)
    sine_part = jnp.sin(twiddle)
    rotated = jnp.stack(
        [
            section_one[0] * cosine + section_one[1] * sine_part,
            section_one[1] * cosine - section_one[0] * sine_part,
        ]
    ).astype(jnp.bfloat16)
    return jnp.einsum(
        "oimj,ispfkm->ospfkj", dft_table(CH_HI), rotated, preferred_element_type=jnp.float32
    ).astype(jnp.bfloat16)


def plain_weights(delays, beam_ids, groups, channel_low, station_total):
    points = CH_LO * CH_HI
    member = (groups[None, :] == (beam_ids % GROUPS)[:, None]).astype(jnp.float32)
    weight_scale = math.sqrt(GROUPS / station_total) * member
    channel = channel_low[:, None] + CH_LO * jnp.arange(CH_HI, dtype=jnp.int32)[None, :]
    fraction = channel.astype(jnp.float32) / float(points)
    phases = TWO_PI * (delays[:, :, None, None] * fraction[None, None])
    weight_re = (weight_scale[:, :, None, None] * jnp.cos(phases)).astype(jnp.bfloat16)
    weight_im = (-weight_scale[:, :, None, None] * jnp.sin(phases)).astype(jnp.bfloat16)
    return (weight_re, weight_im)


def form_beams(weight_re, weight_im, channels):
    real_in = channels[0]
    imag_in = channels[1]

    def contract(weights_part, data_part):
        return jnp.einsum(
            "bsxc,spfxc->bpfxc", weights_part, data_part, preferred_element_type=jnp.float32
        )

    real_out = contract(weight_re, real_in) - contract(weight_im, imag_in)
    imag_out = contract(weight_re, imag_in) + contract(weight_im, real_in)
    return jnp.stack([real_out, imag_out], axis=1)


def select_delays(delay_rows, pointing):
    directions = jnp.arange(delay_rows.shape[0], dtype=jnp.int32)
    onehot = (pointing[:, None] == directions[None, :]).astype(jnp.float32)
    return jnp.dot(
        onehot, delay_rows, precision=lax.Precision.HIGHEST, preferred_element_type=jnp.float32
    )


def with_history(frames_own):
    frame_count = frames_own.shape[3]
    needed = TAPS - 1
    tf_size = lax.axis_size("tf")
    pieces = []
    hop_count = (needed + frame_count - 1) // frame_count
    for hop_step in range(1, hop_count + 1):
        take_count = min(frame_count, needed - (hop_step - 1) * frame_count)
        portion = frames_own[:, :, :, frame_count - take_count :, :]
        pieces.append(passed_along(portion, "tf", hop_step))
    return jnp.concatenate(pieces[::-1] + [frames_own], axis=3)


def plain_body(voltages, delay_table, beam_pointing, station_group):
    planes, stations_here, pol_count, samples_here = voltages.shape
    points = CH_LO * CH_HI
    frame_count = samples_here // points
    frames_own = voltages.reshape(planes, stations_here, pol_count, frame_count, points)
    channels = channelize(with_history(frames_own), frame_count)
    station_total = station_group.shape[0]
    beam_total = beam_pointing.shape[0]
    regrouped = lax.all_to_all(channels, "stn", split_axis=4, concat_axis=1, tiled=True)
    low_count = regrouped.shape[4]
    channel_low = lax.axis_index("stn") * low_count + jnp.arange(low_count, dtype=jnp.int32)
    beam_ids = jnp.arange(beam_total, dtype=jnp.int32)
    delays_all = select_delays(delay_table, beam_pointing)
    weight_re, weight_im = plain_weights(
        delays_all, beam_ids, station_group, channel_low, station_total
    )
    formed = form_beams(weight_re, weight_im, regrouped).astype(jnp.bfloat16)
    result = lax.all_to_all(
        lax.all_to_all(formed, "stn", split_axis=0, concat_axis=4, tiled=True),
        "tf",
        split_axis=4,
        concat_axis=3,
        tiled=True,
    )
    return result


def fits(mesh, voltages, station_group):
    planes, stations, pols, samples = voltages.shape
    tf, stn = mesh.shape["tf"], mesh.shape["stn"]
    frames = samples // POINTS
    return (
        tf == TF and stn == STN and stations == stn * 2 * PER and (planes, pols) == (2, 2)
        and frames % (tf * stn) == 0
    )


def solution(mesh):
    in_specs = (P(None, "stn", None, "tf"), P(), P(), P())
    out_specs = P("stn", None, None, None, "tf", None)

    def whole(*args):
        body = fast_body if fits(mesh, args[0], args[3]) else plain_body
        return jax.shard_map(
            body, mesh=mesh, in_specs=in_specs, out_specs=out_specs, check_vma=False
        )(*args)

    return whole
```

```python
import functools
import math

import jax
import jax.numpy as jnp
import numpy as np
from jax import lax
from jax.experimental import pallas as pl
from jax.experimental.pallas import tpu as pltpu
from jax.sharding import PartitionSpec as P


TAPS = 16
CH_LO = 32
CH_HI = 128
GROUPS = 4
POINTS = CH_LO * CH_HI
TWO_PI = 2.0 * math.pi
BF = jnp.bfloat16
F32 = jnp.float32

LANES = 128
TF = 4
STN = 8
PART = CH_HI // TF
LOW = CH_LO // TF
PER = 4
CHUNKS = 2


def filter_window(position):
    total_len = float(TAPS * POINTS)
    value = position.astype(F32)
    hann_taper = 0.5 - 0.5 * jnp.cos(TWO_PI / total_len * value)
    return jnp.sinc((value - 0.5 * total_len) / float(POINTS)) * hann_taper


def window_rows(part):
    shape = (TAPS, 2 * CH_LO, LANES)
    tap = lax.broadcasted_iota(jnp.int32, shape, 0)
    n2 = lax.broadcasted_iota(jnp.int32, shape, 1) // 2
    n1 = part * PART + lax.broadcasted_iota(jnp.int32, shape, 2) % PART
    return filter_window(tap * POINTS + n2 * CH_HI + n1)


def dft_pair(points):
    counter = np.arange(points)
    angles = TWO_PI / points * (counter[:, None] * counter[None, :] % points)
    factor = 1.0 / math.sqrt(points)
    return np.cos(angles) * factor, np.sin(angles) * factor


def first_table():
    cosine, sine = dft_pair(CH_LO)
    planes = np.stack([np.stack([cosine, sine]), np.stack([-sine, cosine])])
    planes = planes.reshape(2, 2, TF, LOW, CH_LO)
    table = np.einsum("oitkn,pr->otpkinr", planes, np.eye(2))
    return jnp.asarray(table.reshape(4 * CH_LO, 4 * CH_LO), BF)


def second_table():
    cosine, sine = dft_pair(CH_HI)
    table = np.block([[cosine, -sine], [sine, cosine]])
    return jnp.asarray(table, BF)


def twiddle_rows(part):
    shape = (2 * CH_LO, LANES)
    row = lax.broadcasted_iota(jnp.int32, shape, 0)
    k2 = row // (2 * LOW) * LOW + row % LOW
    n1 = part * PART + lax.broadcasted_iota(jnp.int32, shape, 1) % PART
    angle = TWO_PI / POINTS * (k2 * n1).astype(F32)
    return jnp.cos(angle), jnp.sin(angle)


VMEM = pl.BlockSpec(memory_space=pltpu.VMEM)
SMEM = pl.BlockSpec(memory_space=pltpu.SMEM)
HBM = pl.BlockSpec(memory_space=pltpu.HBM)


def params(mib):
    return pltpu.CompilerParams(vmem_limit_bytes=mib << 20)


def cost(mib, flops=0):
    return pl.CostEstimate(flops=flops, bytes_accessed=mib << 20, transcendentals=0)


def swap_lane_blocks(parts):
    lane = lax.broadcasted_iota(jnp.int32, parts[0].shape, 1)
    upper = lane >= 2 * PART
    odd = (lane // PART) % 2 == 1
    turned = [pltpu.roll(part, 2 * PART, 1) for part in parts]
    half = [
        jnp.where(upper, turned[2], parts[0]),
        jnp.where(upper, turned[3], parts[1]),
        jnp.where(upper, parts[2], turned[0]),
        jnp.where(upper, parts[3], turned[1]),
    ]
    out = []
    for low, high in ((half[0], half[1]), (half[2], half[3])):
        out.append(jnp.where(odd, pltpu.roll(high, PART, 1), low))
        out.append(jnp.where(odd, high, pltpu.roll(low, LANES - PART, 1)))
    return out


def spread_kernel(chunk, me_ref, volt_ref, *refs):
    outs, (in_ref, sem) = refs[:TF], refs[TF:]
    planes, _, frames, _, _ = volt_ref.shape
    reads = [
        pltpu.make_async_copy(volt_ref.at[q, pl.ds(chunk * PER, PER)], in_ref.at[q], sem.at[q])
        for q in range(planes)
    ]
    for read in reads:
        read.start()
    for q in range(planes):
        reads[q].wait()
        for me in range(TF):

            @pl.when(me_ref[0] == me)
            def _(me=me, q=q):
                def one(f, carry):
                    parts = [in_ref[q, a, f] for a in range(PER)]
                    for j, block in enumerate(swap_lane_blocks(parts)):
                        outs[j ^ me][q, f] = block
                    return carry

                lax.fori_loop(0, frames, one, 0)


def spread(me, volt, chunk):
    planes, _, frames, rows, _ = volt.shape
    return pl.pallas_call(
        functools.partial(spread_kernel, chunk),
        name="spread",
        in_specs=[SMEM, HBM],
        out_specs=[VMEM] * TF,
        out_shape=[jax.ShapeDtypeStruct((planes, frames, rows, LANES), BF)] * TF,
        scratch_shapes=[
            pltpu.VMEM((planes, PER, frames, rows, LANES), BF),
            pltpu.SemaphoreType.DMA((planes,)),
        ],
        compiler_params=params(6),
        cost_estimate=cost(4),
    )(me, volt)


def channel_kernel(me_ref, *refs):
    sources = refs[:TF]
    win_ref, table_ref, cos_ref, sin_ref, out_ref, stage_ref, filt_ref, done_ref, sem = refs[TF:]
    me = me_ref[0]
    rows = 2 * CH_LO
    history = TAPS - 1
    planes, per_source = sources[0].shape[:2]
    frames = TF * per_source
    for d, ref in enumerate(sources):
        stage_ref[:, pl.ds((me ^ d) * per_source, per_source)] = ref[...]

    strip = 16

    def one_strip(q, step, carry):
        at = pl.multiple_of(step * strip, strip)
        data = [stage_ref[q, f, pl.ds(at, strip), :].astype(F32) for f in range(frames)]
        taps = [win_ref[tap, pl.ds(at, strip), :] for tap in range(TAPS)]
        for f in range(frames):
            total = None
            for tap in range(max(0, history - f), TAPS):
                term = taps[tap] * data[f + tap - history]
                total = term if total is None else total + term
            filt_ref[f, q, pl.ds(at, strip), :] = total.astype(BF)
        return carry

    for q in range(planes):
        lax.fori_loop(0, rows // strip, functools.partial(one_strip, q), 0)

    table = table_ref[...]
    per_dest = frames // STN

    def send(dest):
        return pltpu.make_async_copy(done_ref.at[dest], out_ref.at[dest], sem.at[dest])

    def one_dest(dest, carry):
        cosine, sine = cos_ref[...], sin_ref[...]
        for pair in range(per_dest // 2):
            f = per_dest * dest + 2 * pair
            left = filt_ref[f].reshape(2 * rows, LANES)
            right = filt_ref[f + 1].reshape(2 * rows, LANES)
            both = jnp.concatenate([left, right], axis=1)
            spectrum = jnp.dot(table, both, preferred_element_type=F32)
            for side in range(2):
                real = spectrum[:rows, side * LANES : (side + 1) * LANES]
                imag = spectrum[rows:, side * LANES : (side + 1) * LANES]
                turned = (real * cosine + imag * sine, imag * cosine - real * sine)
                for o in range(2):
                    value = turned[o].astype(BF).reshape(TF, 2 * LOW, LANES)
                    done_ref[dest, :, o, 2 * pair + side] = value
        send(dest).start()
        return carry

    lax.fori_loop(0, STN, one_dest, 0, unroll=2)
    for dest in range(STN):
        send(dest).wait()


def channel_step(me, blocks, window, table, cosine, sine):
    planes, per_source, rows, _ = blocks[0].shape
    frames = TF * per_source
    out = (STN, TF, planes, frames // STN, 2 * LOW, LANES)
    return pl.pallas_call(
        channel_kernel,
        name="channel_step",
        in_specs=[SMEM] + [VMEM] * (TF + 4),
        out_specs=HBM,
        out_shape=jax.ShapeDtypeStruct(out, BF),
        scratch_shapes=[
            pltpu.VMEM((planes, frames, rows, LANES), BF),
            pltpu.VMEM((frames, planes, rows, LANES), BF),
            pltpu.VMEM(out, BF),
            pltpu.SemaphoreType.DMA((STN,)),
        ],
        compiler_params=params(12),
        cost_estimate=cost(8, 1 << 29),
    )(me, *blocks, window, table, cosine, sine)


def weight_kernel(chunk, at_ref, table_ref, beam_ref, group_ref, out_ref, order_ref, start_ref):
    total = group_ref.shape[0]
    members = out_ref.shape[0] - 1
    offsets = out_ref.shape[1]
    scale = math.sqrt(GROUPS / total)
    shape = (LOW, LANES)
    k2 = at_ref[0] * LOW + lax.broadcasted_iota(jnp.int32, shape, 0)
    channel = k2 + CH_LO * lax.broadcasted_iota(jnp.int32, shape, 1)
    fraction = channel.astype(F32) / float(POINTS)

    def station(member):
        return (member // PER) * (PER * CHUNKS) + chunk * PER + member % PER

    def one_member(member, carry):
        s = station(member)
        group = group_ref[s]
        for d in range(offsets):
            beam = group + GROUPS * (at_ref[1] ^ d)
            turns = table_ref[beam_ref[beam], s] * fraction
            quarter = jnp.round(4.0 * turns)
            angle = TWO_PI * (turns - 0.25 * quarter)
            square = angle * angle
            sine = angle * (
                1.0 + square * (-1.0 / 6 + square * (1.0 / 120 + square * (-1.0 / 5040 + square * (1.0 / 362880))))
            )
            cosine = 1.0 + square * (
                -0.5 + square * (1.0 / 24 + square * (-1.0 / 720 + square * (1.0 / 40320)))
            )
            turn = quarter.astype(jnp.int32) & 3
            odd = (turn & 1) == 1
            base_cos = jnp.where(odd, sine, cosine)
            base_sin = jnp.where(odd, cosine, sine)
            real = scale * jnp.where((turn == 1) | (turn == 2), -base_cos, base_cos)
            imag = -scale * jnp.where(turn >= 2, -base_sin, base_sin)
            real = real.astype(BF).astype(F32)
            imag = imag.astype(BF).astype(F32)
            out_ref[member, d, 0] = real
            out_ref[member, d, 1] = imag - real
            out_ref[member, d, 2] = imag + real
        return carry

    lax.fori_loop(0, members, one_member, 0)
    out_ref[members] = jnp.zeros(out_ref.shape[1:], F32)

    at = jnp.int32(0)
    for g in range(GROUPS):
        start_ref[g] = at // 2

        def put(member, at, g=g):
            mine = group_ref[station(member)] == g

            @pl.when(mine)
            def _():
                order_ref[at] = member

            return at + mine.astype(jnp.int32)

        at = lax.fori_loop(0, members, put, at)

        @pl.when(at % 2 == 1)
        def _():
            order_ref[at] = members

        at = at + at % 2
    start_ref[GROUPS] = at // 2


def beam_weights(at, chunk, delay_table, beam_pointing, station_group):
    members = station_group.shape[0] // CHUNKS
    offsets = beam_pointing.shape[0] // GROUPS
    return pl.pallas_call(
        functools.partial(weight_kernel, chunk),
        name="beam_weights",
        in_specs=[SMEM] * 4,
        out_specs=[VMEM, SMEM, SMEM],
        out_shape=[
            jax.ShapeDtypeStruct((members + 1, offsets, 3, LOW, LANES), F32),
            jax.ShapeDtypeStruct((members + GROUPS,), jnp.int32),
            jax.ShapeDtypeStruct((GROUPS + 1,), jnp.int32),
        ],
        compiler_params=params(8),
        cost_estimate=cost(8, 1 << 29),
    )(at, delay_table, beam_pointing, station_group)


def transform(blocks_ref, table_ref, chan_ref):
    sources, _, _, per_dest = blocks_ref.shape[:4]
    rows = per_dest * 2 * LOW
    table = table_ref[...]
    for src in range(sources):
        planes = []
        for o in range(2):
            parts = [blocks_ref[src, j, o].reshape(rows, LANES) for j in range(TF)]
            planes.append(swap_lane_blocks(parts))
        for a in range(PER):
            both = jnp.concatenate([planes[0][a], planes[1][a]], axis=1)
            spectrum = jnp.dot(both, table, preferred_element_type=F32)
            for o in range(2):
                value = spectrum[:, o * LANES : (o + 1) * LANES]
                chan_ref[src * PER + a, o] = value.reshape(per_dest * 2, LOW, LANES)
    chan_ref[chan_ref.shape[0] - 1] = jnp.zeros(chan_ref.shape[1:], F32)


def form_beams_of(offsets, chan_ref, weight_ref, order_ref, start_ref, put):
    count = len(offsets)
    wide = 16 // count
    blocks = chan_ref.shape[2] // wide

    def one_block(step, carry):
        g, base = step // blocks, step % blocks * wide

        def one_pair(pair, acc):
            acc = list(acc)
            for member in (order_ref[2 * pair], order_ref[2 * pair + 1]):
                data = []
                for x in range(wide):
                    re, im = chan_ref[member, 0, base + x], chan_ref[member, 1, base + x]
                    data.append((re + im, re, im))
                for i, d in enumerate(offsets):
                    for y in range(3):
                        weight = weight_ref[member, d, y]
                        for x in range(wide):
                            at = (i * 3 + y) * wide + x
                            acc[at] = acc[at] + weight * data[x][y]
            return tuple(acc)

        zero = jnp.zeros((LOW, LANES), F32)
        acc = lax.fori_loop(start_ref[g], start_ref[g + 1], one_pair, (zero,) * (3 * count * wide))
        for i, d in enumerate(offsets):
            for x in range(wide):
                both, re, im = (acc[(i * 3 + y) * wide + x] for y in range(3))
                put(d, g, 0, base + x, both - im)
                put(d, g, 1, base + x, both + re)
        return carry

    lax.fori_loop(0, GROUPS * blocks, one_block, 0)


def early_kernel(blocks_ref, table_ref, weight_ref, order_ref, start_ref, at_ref, sum_ref, next_ref, chan_ref):
    next_ref[0], next_ref[1] = at_ref[0], at_ref[1]
    transform(blocks_ref, table_ref, chan_ref)

    def put(d, g, o, fp, value):
        sum_ref[d, g, o, fp % 2, fp // 2] = value

    form_beams_of(range(weight_ref.shape[1]), chan_ref, weight_ref, order_ref, start_ref, put)


def late_kernel(offsets, fresh, *refs):
    if fresh:
        blocks_ref, table_ref, weight_ref, order_ref, start_ref, sum_ref = refs[:6]
        chan_ref, outs = refs[6], refs[7:]
        transform(blocks_ref, table_ref, chan_ref)
    else:
        chan_ref, weight_ref, order_ref, start_ref, sum_ref = refs[:5]
        outs = refs[5:]

    def put(d, g, o, fp, value):
        f, p = fp // 2, fp % 2
        outs[d - offsets[0]][g, o, p, f] = (value + sum_ref[d, g, o, p, f]).astype(BF)

    form_beams_of(offsets, chan_ref, weight_ref, order_ref, start_ref, put)


def beam_shapes(blocks, weights):
    planes, per_dest = blocks.shape[2:4]
    one = (GROUPS, planes, 2, per_dest, LOW, LANES)
    return one, (weights.shape[0], planes, 2 * per_dest, LOW, LANES)


def beams_early(blocks, table, weights, order, start, at):
    one, chan = beam_shapes(blocks, weights)
    return pl.pallas_call(
        early_kernel,
        name="beams_early",
        in_specs=[VMEM] * 3 + [SMEM] * 3,
        out_specs=[VMEM, SMEM],
        out_shape=[
            jax.ShapeDtypeStruct((weights.shape[1],) + one, F32),
            jax.ShapeDtypeStruct(at.shape, at.dtype),
        ],
        scratch_shapes=[pltpu.VMEM(chan, F32)],
        compiler_params=params(12),
        cost_estimate=cost(8, 1 << 29),
    )(blocks, table, weights, order, start, at)


def beams_far(blocks, table, weights, order, start, partial):
    one, chan = beam_shapes(blocks, weights)
    offsets = range(weights.shape[1] // 2, weights.shape[1])
    outs = pl.pallas_call(
        functools.partial(late_kernel, offsets, True),
        name="beams_far",
        in_specs=[VMEM] * 3 + [SMEM] * 2 + [VMEM],
        out_specs=[VMEM] * (1 + len(offsets)),
        out_shape=[jax.ShapeDtypeStruct(chan, F32)] + [jax.ShapeDtypeStruct(one, BF)] * len(offsets),
        compiler_params=params(12),
        cost_estimate=cost(8, 1 << 29),
    )(blocks, table, weights, order, start, partial)
    return outs[0], outs[1:]


def beams_near(chan, weights, order, start, partial):
    offsets = range(weights.shape[1] // 2)
    return pl.pallas_call(
        functools.partial(late_kernel, offsets, False),
        name="beams_near",
        in_specs=[VMEM] * 2 + [SMEM] * 2 + [VMEM],
        out_specs=[VMEM] * len(offsets),
        out_shape=[jax.ShapeDtypeStruct(partial.shape[1:], BF)] * len(offsets),
        compiler_params=params(12),
        cost_estimate=cost(8, 1 << 29),
    )(chan, weights, order, start, partial)


def gather_kernel(me_ref, *refs):
    parts, out_ref, sem = refs[:STN], refs[STN], refs[STN + 1]
    per_dest = parts[0].shape[3]
    copies = []
    for d, part in enumerate(parts):
        frames = pl.ds((me_ref[0] ^ d) * per_dest, per_dest)
        copies.append(pltpu.make_async_copy(part, out_ref.at[:, :, :, frames], sem.at[d]))
    for copy in copies:
        copy.start()
    for copy in copies:
        copy.wait()


def gather_frames(me, parts):
    shape = parts[0].shape
    shape = shape[:3] + (shape[3] * len(parts),) + shape[4:]
    return pl.pallas_call(
        gather_kernel,
        name="gather_frames",
        in_specs=[SMEM] + [VMEM] * len(parts),
        out_specs=pl.BlockSpec(memory_space=pl.ANY),
        out_shape=jax.ShapeDtypeStruct(shape, BF),
        scratch_shapes=[pltpu.SemaphoreType.DMA((len(parts),))],
        compiler_params=params(4),
    )(me, *parts)


def swapped(value, axis, offset):
    count = lax.axis_size(axis)
    return lax.ppermute(value, axis, [(i, i ^ offset) for i in range(count)])


def fast_body(voltages, delay_table, beam_pointing, station_group):
    planes, stations_here, pols, samples_here = voltages.shape
    part, home = lax.axis_index("tf"), lax.axis_index("stn")
    me = part.astype(jnp.int32).reshape(1)
    owner = home.astype(jnp.int32).reshape(1)
    at = jnp.concatenate([me, owner])
    rows = samples_here // LANES
    volt = voltages.reshape(planes, stations_here, pols, rows, LANES)
    volt = volt.transpose(0, 1, 3, 2, 4)
    volt = volt.reshape(planes, stations_here, rows // CH_LO, CH_LO * pols, LANES)
    cosine, sine = twiddle_rows(part)
    window, first, second = window_rows(part), first_table(), second_table()

    blocks = []
    for chunk in range(CHUNKS):
        own = spread(me, volt, chunk)
        row = [own[0]]
        for d in range(1, TF):
            row.append(swapped(own[d], "tf", d))
        blocks.append(row)

    turned = []
    for chunk in range(CHUNKS):
        value = channel_step(me, blocks[chunk], window, first, cosine, sine)
        shape = value.shape
        value = value.reshape((STN * TF,) + shape[2:])
        value = lax.all_to_all(value, ("stn", "tf"), split_axis=0, concat_axis=0, tiled=True)
        turned.append(value.reshape(shape))

    args = (delay_table, beam_pointing, station_group)
    weights = beam_weights(at, 0, *args)
    partial, at = beams_early(turned[0], second, *weights, at)
    weights = beam_weights(at, 1, *args)
    chan, far = beams_far(turned[1], second, *weights, partial)
    parts = [None] * STN
    for i, value in enumerate(far):
        d = STN // 2 + i
        parts[d] = swapped(value, "stn", d)
    near = beams_near(chan, *weights, partial)
    for d, value in enumerate(near):
        parts[d] = swapped(value, "stn", d) if d else value
    return gather_frames(owner, parts)


def passed_along(value, axis, steps):
    count = lax.axis_size(axis)
    first, last = (max(0, -steps), min(count, count - steps))
    return lax.ppermute(value, axis, [(source, source + steps) for source in range(first, last)])


def plain_window(tap_count, points):
    position = jnp.arange(tap_count * points, dtype=jnp.int32).astype(jnp.float32)
    total_len = float(tap_count * points)
    hann_taper = 0.5 - 0.5 * jnp.cos(TWO_PI / total_len * position)
    kernel = jnp.sinc((position - 0.5 * total_len) / float(points)) * hann_taper
    return kernel.reshape(tap_count, points)


def dft_table(points):
    counter = jnp.arange(points, dtype=jnp.int32)
    product = counter[:, None] * counter[None, :] % points
    angles = TWO_PI / points * product.astype(jnp.float32)
    factor = 1.0 / math.sqrt(points)
    cosine = jnp.cos(angles) * factor
    sine_part = jnp.sin(angles) * factor
    stacked = jnp.stack([jnp.stack([cosine, sine_part]), jnp.stack([-sine_part, cosine])])
    return stacked.astype(jnp.bfloat16)


def channelize(extended, frame_count):
    points = CH_LO * CH_HI
    window = plain_window(TAPS, points)
    filtered = sum(
        (
            window[tap_step]
            * extended[:, :, :, tap_step : tap_step + frame_count, :].astype(jnp.float32)
            for tap_step in range(TAPS)
        )
    )
    filtered = filtered.astype(jnp.bfloat16)
    shaped = filtered.reshape(filtered.shape[:4] + (CH_LO, CH_HI))
    section_one = jnp.einsum(
        "oikn,ispfnm->ospfkm", dft_table(CH_LO), shaped, preferred_element_type=jnp.float32
    )
    low_index = jnp.arange(CH_LO, dtype=jnp.int32)
    high_index = jnp.arange(CH_HI, dtype=jnp.int32)
    twiddle = TWO_PI / points * (low_index[:, None] * high_index[None, :]).astype(jnp.float32)
    cosine = jnp.cos(twiddle)
    sine_part = jnp.sin(twiddle)
    rotated = jnp.stack(
        [
            section_one[0] * cosine + section_one[1] * sine_part,
            section_one[1] * cosine - section_one[0] * sine_part,
        ]
    ).astype(jnp.bfloat16)
    return jnp.einsum(
        "oimj,ispfkm->ospfkj", dft_table(CH_HI), rotated, preferred_element_type=jnp.float32
    ).astype(jnp.bfloat16)


def plain_weights(delays, beam_ids, groups, channel_low, station_total):
    points = CH_LO * CH_HI
    member = (groups[None, :] == (beam_ids % GROUPS)[:, None]).astype(jnp.float32)
    weight_scale = math.sqrt(GROUPS / station_total) * member
    channel = channel_low[:, None] + CH_LO * jnp.arange(CH_HI, dtype=jnp.int32)[None, :]
    fraction = channel.astype(jnp.float32) / float(points)
    phases = TWO_PI * (delays[:, :, None, None] * fraction[None, None])
    weight_re = (weight_scale[:, :, None, None] * jnp.cos(phases)).astype(jnp.bfloat16)
    weight_im = (-weight_scale[:, :, None, None] * jnp.sin(phases)).astype(jnp.bfloat16)
    return (weight_re, weight_im)


def form_beams(weight_re, weight_im, channels):
    real_in = channels[0]
    imag_in = channels[1]

    def contract(weights_part, data_part):
        return jnp.einsum(
            "bsxc,spfxc->bpfxc", weights_part, data_part, preferred_element_type=jnp.float32
        )

    real_out = contract(weight_re, real_in) - contract(weight_im, imag_in)
    imag_out = contract(weight_re, imag_in) + contract(weight_im, real_in)
    return jnp.stack([real_out, imag_out], axis=1)


def select_delays(delay_rows, pointing):
    directions = jnp.arange(delay_rows.shape[0], dtype=jnp.int32)
    onehot = (pointing[:, None] == directions[None, :]).astype(jnp.float32)
    return jnp.dot(
        onehot, delay_rows, precision=lax.Precision.HIGHEST, preferred_element_type=jnp.float32
    )


def with_history(frames_own):
    frame_count = frames_own.shape[3]
    needed = TAPS - 1
    pieces = []
    hop_count = (needed + frame_count - 1) // frame_count
    for hop_step in range(1, hop_count + 1):
        take_count = min(frame_count, needed - (hop_step - 1) * frame_count)
        portion = frames_own[:, :, :, frame_count - take_count :, :]
        pieces.append(passed_along(portion, "tf", hop_step))
    return jnp.concatenate(pieces[::-1] + [frames_own], axis=3)


def plain_body(voltages, delay_table, beam_pointing, station_group):
    planes, stations_here, pol_count, samples_here = voltages.shape
    points = CH_LO * CH_HI
    frame_count = samples_here // points
    frames_own = voltages.reshape(planes, stations_here, pol_count, frame_count, points)
    channels = channelize(with_history(frames_own), frame_count)
    station_total = station_group.shape[0]
    beam_total = beam_pointing.shape[0]
    regrouped = lax.all_to_all(channels, "stn", split_axis=4, concat_axis=1, tiled=True)
    low_count = regrouped.shape[4]
    channel_low = lax.axis_index("stn") * low_count + jnp.arange(low_count, dtype=jnp.int32)
    beam_ids = jnp.arange(beam_total, dtype=jnp.int32)
    delays_all = select_delays(delay_table, beam_pointing)
    weight_re, weight_im = plain_weights(
        delays_all, beam_ids, station_group, channel_low, station_total
    )
    formed = form_beams(weight_re, weight_im, regrouped).astype(jnp.bfloat16)
    result = lax.all_to_all(
        lax.all_to_all(formed, "stn", split_axis=0, concat_axis=4, tiled=True),
        "tf",
        split_axis=4,
        concat_axis=3,
        tiled=True,
    )
    return result


def solution(mesh):
    in_specs = (P(None, "stn", None, "tf"), P(), P(), P())
    out_specs = P("stn", None, None, None, "tf", None)

    def spread_over(body):
        return jax.shard_map(
            body, mesh=mesh, in_specs=in_specs, out_specs=out_specs, check_vma=False
        )

    if mesh.shape["tf"] == TF and mesh.shape["stn"] == STN:
        return spread_over(fast_body)
    return spread_over(plain_body)
```

```python
import functools
import math

import jax
import jax.numpy as jnp
import numpy as np
from jax import lax
from jax.experimental import pallas as pl
from jax.experimental.pallas import tpu as pltpu
from jax.sharding import PartitionSpec as P


TAPS = 16
CH_LO = 32
CH_HI = 128
GROUPS = 4
POINTS = CH_LO * CH_HI
TWO_PI = 2.0 * math.pi
BF = jnp.bfloat16
F32 = jnp.float32

LANES = 128
TF = 4
STN = 8
PART = CH_HI // TF
LOW = CH_LO // TF
PER = 4
CHUNKS = 2


def filter_window(position):
    total_len = float(TAPS * POINTS)
    value = position.astype(F32)
    hann_taper = 0.5 - 0.5 * jnp.cos(TWO_PI / total_len * value)
    return jnp.sinc((value - 0.5 * total_len) / float(POINTS)) * hann_taper


def window_rows(part):
    shape = (TAPS, 2 * CH_LO, LANES)
    tap = lax.broadcasted_iota(jnp.int32, shape, 0)
    n2 = lax.broadcasted_iota(jnp.int32, shape, 1) // 2
    n1 = part * PART + lax.broadcasted_iota(jnp.int32, shape, 2) % PART
    return filter_window(tap * POINTS + n2 * CH_HI + n1)


def dft_pair(points):
    counter = np.arange(points)
    angles = TWO_PI / points * (counter[:, None] * counter[None, :] % points)
    factor = 1.0 / math.sqrt(points)
    return np.cos(angles) * factor, np.sin(angles) * factor


def first_table():
    cosine, sine = dft_pair(CH_LO)
    planes = np.stack([np.stack([cosine, sine]), np.stack([-sine, cosine])])
    planes = planes.reshape(2, 2, TF, LOW, CH_LO)
    table = np.einsum("oitkn,pr->otpkinr", planes, np.eye(2))
    return jnp.asarray(table.reshape(2, TF, 2 * LOW, 4 * CH_LO), BF)


def second_table():
    cosine, sine = dft_pair(CH_HI)
    table = np.block([[cosine, -sine], [sine, cosine]])
    return jnp.asarray(table.reshape(2, TF, PART, 2 * CH_HI), BF)


def twiddle_rows(part):
    shape = (TF, 2 * LOW, LANES)
    k2 = lax.broadcasted_iota(jnp.int32, shape, 0) * LOW
    k2 = k2 + lax.broadcasted_iota(jnp.int32, shape, 1) % LOW
    n1 = part * PART + lax.broadcasted_iota(jnp.int32, shape, 2) % PART
    angle = TWO_PI / POINTS * (k2 * n1).astype(F32)
    return jnp.cos(angle), jnp.sin(angle)


VMEM = pl.BlockSpec(memory_space=pltpu.VMEM)
SMEM = pl.BlockSpec(memory_space=pltpu.SMEM)
HBM = pl.BlockSpec(memory_space=pltpu.HBM)


def params(mib):
    return pltpu.CompilerParams(vmem_limit_bytes=mib << 20)


def cost(mib, flops=0):
    return pl.CostEstimate(flops=flops, bytes_accessed=mib << 20, transcendentals=0)


def swap_lane_blocks(parts):
    lane = lax.broadcasted_iota(jnp.int32, parts[0].shape, 1)
    upper = lane >= 2 * PART
    odd = (lane // PART) % 2 == 1
    turned = [pltpu.roll(part, 2 * PART, 1) for part in parts]
    half = [
        jnp.where(upper, turned[2], parts[0]),
        jnp.where(upper, turned[3], parts[1]),
        jnp.where(upper, parts[2], turned[0]),
        jnp.where(upper, parts[3], turned[1]),
    ]
    out = []
    for low, high in ((half[0], half[1]), (half[2], half[3])):
        out.append(jnp.where(odd, pltpu.roll(high, PART, 1), low))
        out.append(jnp.where(odd, high, pltpu.roll(low, LANES - PART, 1)))
    return out


def spread_kernel(chunk, me_ref, volt_ref, *outs):
    planes, _, frames = volt_ref.shape[:3]
    for me in range(TF):

        @pl.when(me_ref[0] == me)
        def _(me=me):
            def one(step, carry):
                q, f = step // frames, step % frames
                parts = [volt_ref[q, chunk * PER + a, f] for a in range(PER)]
                for j, block in enumerate(swap_lane_blocks(parts)):
                    outs[j ^ me][q, f] = block
                return carry

            lax.fori_loop(0, planes * frames, one, 0, unroll=2)


def spread(me, volt, chunk):
    planes, _, frames, rows, _ = volt.shape
    return pl.pallas_call(
        functools.partial(spread_kernel, chunk),
        name="spread",
        in_specs=[SMEM, VMEM],
        out_specs=[VMEM] * TF,
        out_shape=[jax.ShapeDtypeStruct((planes, frames, rows, LANES), BF)] * TF,
        compiler_params=params(2),
        cost_estimate=cost(4),
    )(me, volt)


def channel_kernel(split, me_ref, *refs):
    sources = refs[:TF]
    win_ref, table_ref, cos_ref, sin_ref = refs[TF : TF + 4]
    stage_ref, filt_ref = refs[-2:] if split else refs[-4:-2]
    me = me_ref[0]
    rows = 2 * CH_LO
    history = TAPS - 1
    planes, per_source = sources[0].shape[:2]
    frames = TF * per_source
    for d, ref in enumerate(sources):
        stage_ref[:, pl.ds((me ^ d) * per_source, per_source)] = ref[...]

    strip = 16

    def one_strip(q, step, carry):
        at = pl.multiple_of(step * strip, strip)
        data = [stage_ref[q, f, pl.ds(at, strip), :].astype(F32) for f in range(frames)]
        taps = [win_ref[tap, pl.ds(at, strip), :] for tap in range(TAPS)]
        for f in range(frames):
            total = None
            for tap in range(max(0, history - f), TAPS):
                term = taps[tap] * data[f + tap - history]
                total = term if total is None else total + term
            filt_ref[f, q, pl.ds(at, strip), :] = total.astype(BF)
        return carry

    for q in range(planes):
        lax.fori_loop(0, rows // strip, functools.partial(one_strip, q), 0)

    ranges = [(me ^ t) if split else t for t in range(TF)]
    table = jnp.concatenate([table_ref[o, t] for o in range(planes) for t in ranges], axis=0)
    per_dest = frames // STN
    if split:
        outs = refs[TF + 4 : TF + 4 + TF]
    else:
        out_ref, done_ref, sem = refs[TF + 4], refs[-2], refs[-1]

        def send(dest):
            return pltpu.make_async_copy(done_ref.at[dest], out_ref.at[dest], sem.at[dest])

    def one_dest(dest, carry):
        cosine = jnp.concatenate([cos_ref[t] for t in ranges], axis=0)
        sine = jnp.concatenate([sin_ref[t] for t in ranges], axis=0)
        for pair in range(per_dest // 2):
            f = per_dest * dest + 2 * pair
            left = filt_ref[f].reshape(2 * rows, LANES)
            right = filt_ref[f + 1].reshape(2 * rows, LANES)
            both = jnp.concatenate([left, right], axis=1)
            spectrum = jnp.dot(table, both, preferred_element_type=F32)
            for side in range(2):
                real = spectrum[:rows, side * LANES : (side + 1) * LANES]
                imag = spectrum[rows:, side * LANES : (side + 1) * LANES]
                turned = (real * cosine + imag * sine, imag * cosine - real * sine)
                for o in range(2):
                    value = turned[o].astype(BF).reshape(TF, 2 * LOW, LANES)
                    if split:
                        for d in range(TF):
                            outs[d][dest, o, 2 * pair + side] = value[d]
                    else:
                        done_ref[dest, :, o, 2 * pair + side] = value
        if not split:
            send(dest).start()
        return carry

    lax.fori_loop(0, STN, one_dest, 0, unroll=2)
    if not split:
        for dest in range(STN):
            send(dest).wait()


def channel_step(me, blocks, window, table, cosine, sine, split):
    planes, per_source, rows, _ = blocks[0].shape
    frames = TF * per_source
    tail = (planes, frames // STN, 2 * LOW, LANES)
    scratch = [
        pltpu.VMEM((planes, frames, rows, LANES), BF),
        pltpu.VMEM((frames, planes, rows, LANES), BF),
    ]
    if split:
        out_shape = [jax.ShapeDtypeStruct((STN,) + tail, BF)] * TF
        out_specs = [VMEM] * TF
    else:
        out = (STN, TF) + tail
        out_shape, out_specs = jax.ShapeDtypeStruct(out, BF), HBM
        scratch += [pltpu.VMEM(out, BF), pltpu.SemaphoreType.DMA((STN,))]
    return pl.pallas_call(
        functools.partial(channel_kernel, split),
        name="channel_step",
        in_specs=[SMEM] + [VMEM] * (TF + 4),
        out_specs=out_specs,
        out_shape=out_shape,
        scratch_shapes=scratch,
        compiler_params=params(12),
        cost_estimate=cost(8, 1 << 29),
    )(me, *blocks, window, table, cosine, sine)


def weight_kernel(chunk, at_ref, table_ref, beam_ref, group_ref, out_ref, order_ref, start_ref):
    total = group_ref.shape[0]
    members = out_ref.shape[0] - 1
    offsets = out_ref.shape[1]
    scale = math.sqrt(GROUPS / total)
    shape = (LOW, LANES)
    k2 = at_ref[0] * LOW + lax.broadcasted_iota(jnp.int32, shape, 0)
    channel = k2 + CH_LO * lax.broadcasted_iota(jnp.int32, shape, 1)
    fraction = channel.astype(F32) / float(POINTS)

    def station(member):
        source = member // PER
        if chunk:
            source = source ^ at_ref[1]
        return source * (PER * CHUNKS) + chunk * PER + member % PER

    def one_member(member, carry):
        s = station(member)
        group = group_ref[s]
        for d in range(offsets):
            beam = group + GROUPS * (at_ref[1] ^ d)
            turns = table_ref[beam_ref[beam], s] * fraction
            quarter = jnp.round(4.0 * turns)
            angle = TWO_PI * (turns - 0.25 * quarter)
            square = angle * angle
            sine = angle * (
                1.0 + square * (-1.0 / 6 + square * (1.0 / 120 + square * (-1.0 / 5040 + square * (1.0 / 362880))))
            )
            cosine = 1.0 + square * (
                -0.5 + square * (1.0 / 24 + square * (-1.0 / 720 + square * (1.0 / 40320)))
            )
            turn = quarter.astype(jnp.int32) & 3
            odd = (turn & 1) == 1
            base_cos = jnp.where(odd, sine, cosine)
            base_sin = jnp.where(odd, cosine, sine)
            real = scale * jnp.where((turn == 1) | (turn == 2), -base_cos, base_cos)
            imag = -scale * jnp.where(turn >= 2, -base_sin, base_sin)
            real = real.astype(BF).astype(F32)
            imag = imag.astype(BF).astype(F32)
            out_ref[member, d, 0] = real
            out_ref[member, d, 1] = imag - real
            out_ref[member, d, 2] = imag + real
        return carry

    lax.fori_loop(0, members, one_member, 0)
    out_ref[members] = jnp.zeros(out_ref.shape[1:], F32)

    at = jnp.int32(0)
    for g in range(GROUPS):
        start_ref[g] = at // 2

        def put(member, at, g=g):
            mine = group_ref[station(member)] == g

            @pl.when(mine)
            def _():
                order_ref[at] = member

            return at + mine.astype(jnp.int32)

        at = lax.fori_loop(0, members, put, at)

        @pl.when(at % 2 == 1)
        def _():
            order_ref[at] = members

        at = at + at % 2
    start_ref[GROUPS] = at // 2


def beam_weights(at, chunk, delay_table, beam_pointing, station_group):
    members = station_group.shape[0] // CHUNKS
    offsets = beam_pointing.shape[0] // GROUPS
    return pl.pallas_call(
        functools.partial(weight_kernel, chunk),
        name="beam_weights",
        in_specs=[SMEM] * 4,
        out_specs=[VMEM, SMEM, SMEM],
        out_shape=[
            jax.ShapeDtypeStruct((members + 1, offsets, 3, LOW, LANES), F32),
            jax.ShapeDtypeStruct((members + GROUPS,), jnp.int32),
            jax.ShapeDtypeStruct((GROUPS + 1,), jnp.int32),
        ],
        compiler_params=params(8),
        cost_estimate=cost(8, 1 << 29),
    )(at, delay_table, beam_pointing, station_group)


def transform(parts_of, table, put):
    planes = [swap_lane_blocks(parts_of(o)) for o in range(2)]
    for a in range(PER):
        both = jnp.concatenate([planes[0][a], planes[1][a]], axis=1)
        spectrum = jnp.dot(both, table, preferred_element_type=F32)
        for o in range(2):
            put(a, o, spectrum[:, o * LANES : (o + 1) * LANES])


def table_of(table_ref, parts):
    return jnp.concatenate([table_ref[q, j] for q in range(2) for j in parts], axis=0)


def middle_kernel(at_ref, *refs):
    blocks, table_ref, outs = refs[:TF], refs[TF], refs[TF + 1 :]
    me, owner = at_ref[0], at_ref[1]
    per_dest = blocks[0].shape[2]
    table = table_of(table_ref, [me ^ d for d in range(TF)])
    for e, out in enumerate(outs):

        def parts_of(o, e=e):
            return [block[owner ^ e, o].reshape(per_dest * 2 * LOW, LANES) for block in blocks]

        def put(a, o, value, out=out):
            out[a, o] = value.astype(BF)

        transform(parts_of, table, put)


def middle_step(at, blocks, table):
    _, planes, per_dest, _, _ = blocks[0].shape
    out = (PER, planes, per_dest * 2 * LOW, LANES)
    return pl.pallas_call(
        middle_kernel,
        name="middle_step",
        in_specs=[SMEM] + [VMEM] * (TF + 1),
        out_specs=[VMEM] * STN,
        out_shape=[jax.ShapeDtypeStruct(out, BF)] * STN,
        compiler_params=params(4),
        cost_estimate=cost(4, 1 << 28),
    )(at, *blocks, table)


def form_beams_of(offsets, chan_ref, weight_ref, order_ref, start_ref, put):
    count = len(offsets)
    wide = 16 // count
    blocks = chan_ref.shape[2] // wide

    def one_block(step, carry):
        g, base = step // blocks, step % blocks * wide

        def one_pair(pair, acc):
            acc = list(acc)
            for member in (order_ref[2 * pair], order_ref[2 * pair + 1]):
                data = []
                for x in range(wide):
                    re, im = chan_ref[member, 0, base + x], chan_ref[member, 1, base + x]
                    data.append((re + im, re, im))
                for i, d in enumerate(offsets):
                    for y in range(3):
                        weight = weight_ref[member, d, y]
                        for x in range(wide):
                            at = (i * 3 + y) * wide + x
                            acc[at] = acc[at] + weight * data[x][y]
            return tuple(acc)

        zero = jnp.zeros((LOW, LANES), F32)
        acc = lax.fori_loop(start_ref[g], start_ref[g + 1], one_pair, (zero,) * (3 * count * wide))
        for i, d in enumerate(offsets):
            for x in range(wide):
                both, re, im = (acc[(i * 3 + y) * wide + x] for y in range(3))
                put(d, g, 0, base + x, both - im)
                put(d, g, 1, base + x, both + re)
        return carry

    lax.fori_loop(0, GROUPS * blocks, one_block, 0)


def early_kernel(blocks_ref, table_ref, weight_ref, order_ref, start_ref, sum_hbm, chan_ref, sum_ref, sem):
    sources, _, _, per_dest = blocks_ref.shape[:4]
    table = table_of(table_ref, range(TF))
    for src in range(sources):

        def parts_of(o, src=src):
            return [blocks_ref[src, j, o].reshape(per_dest * 2 * LOW, LANES) for j in range(TF)]

        def put(a, o, value, src=src):
            chan_ref[src * PER + a, o] = value.reshape(per_dest * 2, LOW, LANES)

        transform(parts_of, table, put)
    chan_ref[chan_ref.shape[0] - 1] = jnp.zeros(chan_ref.shape[1:], F32)

    def keep(d, g, o, fp, value):
        sum_ref[d, g, o, fp % 2, fp // 2] = value

    form_beams_of(range(weight_ref.shape[1]), chan_ref, weight_ref, order_ref, start_ref, keep)
    write = pltpu.make_async_copy(sum_ref, sum_hbm, sem)
    write.start()
    write.wait()


def late_kernel(offsets, fresh, weight_ref, order_ref, start_ref, sum_hbm, *refs):
    sum_ref, sem = refs[-2:]
    read = pltpu.make_async_copy(sum_hbm.at[pl.ds(offsets[0], len(offsets))], sum_ref, sem)
    read.start()
    if fresh:
        blocks, chan_ref, outs = refs[:STN], refs[STN], refs[STN + 1 : -2]
        members, planes, both = chan_ref.shape[:3]
        for e, block in enumerate(blocks):
            value = block[...].astype(F32)
            chan_ref[pl.ds(e * PER, PER)] = value.reshape(PER, planes, both, LOW, LANES)
        chan_ref[members - 1] = jnp.zeros(chan_ref.shape[1:], F32)
    else:
        chan_ref, outs = refs[0], refs[1:-2]
    read.wait()

    def put(d, g, o, fp, value):
        f, p = fp // 2, fp % 2
        at = d - offsets[0]
        outs[at][g, o, p, f] = (value + sum_ref[at, g, o, p, f]).astype(BF)

    form_beams_of(offsets, chan_ref, weight_ref, order_ref, start_ref, put)


def beams_early(blocks, table, weights, order, start):
    planes, per_dest = blocks.shape[2:4]
    out = (weights.shape[1], GROUPS, planes, 2, per_dest, LOW, LANES)
    return pl.pallas_call(
        early_kernel,
        name="beams_early",
        in_specs=[VMEM] * 3 + [SMEM] * 2,
        out_specs=HBM,
        out_shape=jax.ShapeDtypeStruct(out, F32),
        scratch_shapes=[
            pltpu.VMEM((weights.shape[0], planes, 2 * per_dest, LOW, LANES), F32),
            pltpu.VMEM(out, F32),
            pltpu.SemaphoreType.DMA,
        ],
        compiler_params=params(12),
        cost_estimate=cost(8, 1 << 29),
    )(blocks, table, weights, order, start)


def beams_late(offsets, blocks, weights, order, start, partial):
    fresh = isinstance(blocks, list)
    more = blocks if fresh else [blocks]
    one = partial.shape[1:]
    out_shape = [jax.ShapeDtypeStruct(one, BF)] * len(offsets)
    if fresh:
        chan = (weights.shape[0], one[1], one[2] * one[3], LOW, LANES)
        out_shape = [jax.ShapeDtypeStruct(chan, F32)] + out_shape
    return pl.pallas_call(
        functools.partial(late_kernel, offsets, fresh),
        name="beams_late",
        in_specs=[VMEM, SMEM, SMEM, HBM] + [VMEM] * len(more),
        out_specs=[VMEM] * len(out_shape),
        out_shape=out_shape,
        scratch_shapes=[pltpu.VMEM((len(offsets),) + one, F32), pltpu.SemaphoreType.DMA],
        compiler_params=params(12),
        cost_estimate=cost(8, 1 << 29),
    )(weights, order, start, partial, *more)


def gather_kernel(me_ref, *refs):
    parts, out_ref, sem = refs[:STN], refs[STN], refs[STN + 1]
    per_dest = parts[0].shape[3]
    copies = []
    for d, part in enumerate(parts):
        frames = pl.ds((me_ref[0] ^ d) * per_dest, per_dest)
        copies.append(pltpu.make_async_copy(part, out_ref.at[:, :, :, frames], sem.at[d]))
    for copy in copies:
        copy.start()
    for copy in copies:
        copy.wait()


def gather_frames(me, parts):
    shape = parts[0].shape
    shape = shape[:3] + (shape[3] * len(parts),) + shape[4:]
    return pl.pallas_call(
        gather_kernel,
        name="gather_frames",
        in_specs=[SMEM] + [VMEM] * len(parts),
        out_specs=pl.BlockSpec(memory_space=pl.ANY),
        out_shape=jax.ShapeDtypeStruct(shape, BF),
        scratch_shapes=[pltpu.SemaphoreType.DMA((len(parts),))],
        compiler_params=params(4),
    )(me, *parts)


def swapped(value, axis, offset):
    count = lax.axis_size(axis)
    return lax.ppermute(value, axis, [(i, i ^ offset) for i in range(count)])


def fast_body(voltages, delay_table, beam_pointing, station_group):
    planes, stations_here, pols, samples_here = voltages.shape
    part, home = lax.axis_index("tf"), lax.axis_index("stn")
    me = part.astype(jnp.int32).reshape(1)
    owner = home.astype(jnp.int32).reshape(1)
    at = jnp.concatenate([me, owner])
    rows = samples_here // LANES
    volt = voltages.reshape(planes, stations_here, pols, rows, LANES)
    volt = volt.transpose(0, 1, 3, 2, 4)
    volt = volt.reshape(planes, stations_here, rows // CH_LO, CH_LO * pols, LANES)
    cosine, sine = twiddle_rows(part)
    window, first, second = window_rows(part), first_table(), second_table()

    blocks = []
    for chunk in range(CHUNKS):
        own = spread(me, volt, chunk)
        row = [own[0]]
        for d in range(1, TF):
            row.append(swapped(own[d], "tf", d))
        blocks.append(row)

    value = channel_step(me, blocks[0], window, first, cosine, sine, False)
    shape = value.shape
    value = value.reshape((STN * TF,) + shape[2:])
    value = lax.all_to_all(value, ("stn", "tf"), split_axis=0, concat_axis=0, tiled=True)
    turned = value.reshape(shape)

    own = channel_step(me, blocks[1], window, first, cosine, sine, True)
    row = [own[0]]
    for d in range(1, TF):
        row.append(swapped(own[d], "tf", d))
    own = middle_step(at, row, second)
    late = [own[0]]
    for e in range(1, STN):
        late.append(swapped(own[e], "stn", e))

    args = (delay_table, beam_pointing, station_group)
    weights = beam_weights(at, 0, *args)
    partial = beams_early(turned, second, *weights)
    weights = beam_weights(at, 1, *args)
    chan, *far = beams_late(range(STN // 2, STN), late, *weights, partial)
    parts = [None] * STN
    for i, value in enumerate(far):
        d = STN // 2 + i
        parts[d] = swapped(value, "stn", d)
    near = beams_late(range(STN // 2), chan, *weights, partial)
    for d, value in enumerate(near):
        parts[d] = swapped(value, "stn", d) if d else value
    return gather_frames(owner, parts)


def passed_along(value, axis, steps):
    count = lax.axis_size(axis)
    first, last = (max(0, -steps), min(count, count - steps))
    return lax.ppermute(value, axis, [(source, source + steps) for source in range(first, last)])


def plain_window(tap_count, points):
    position = jnp.arange(tap_count * points, dtype=jnp.int32).astype(jnp.float32)
    total_len = float(tap_count * points)
    hann_taper = 0.5 - 0.5 * jnp.cos(TWO_PI / total_len * position)
    kernel = jnp.sinc((position - 0.5 * total_len) / float(points)) * hann_taper
    return kernel.reshape(tap_count, points)


def dft_table(points):
    counter = jnp.arange(points, dtype=jnp.int32)
    product = counter[:, None] * counter[None, :] % points
    angles = TWO_PI / points * product.astype(jnp.float32)
    factor = 1.0 / math.sqrt(points)
    cosine = jnp.cos(angles) * factor
    sine_part = jnp.sin(angles) * factor
    stacked = jnp.stack([jnp.stack([cosine, sine_part]), jnp.stack([-sine_part, cosine])])
    return stacked.astype(jnp.bfloat16)


def channelize(extended, frame_count):
    points = CH_LO * CH_HI
    window = plain_window(TAPS, points)
    filtered = sum(
        (
            window[tap_step]
            * extended[:, :, :, tap_step : tap_step + frame_count, :].astype(jnp.float32)
            for tap_step in range(TAPS)
        )
    )
    filtered = filtered.astype(jnp.bfloat16)
    shaped = filtered.reshape(filtered.shape[:4] + (CH_LO, CH_HI))
    section_one = jnp.einsum(
        "oikn,ispfnm->ospfkm", dft_table(CH_LO), shaped, preferred_element_type=jnp.float32
    )
    low_index = jnp.arange(CH_LO, dtype=jnp.int32)
    high_index = jnp.arange(CH_HI, dtype=jnp.int32)
    twiddle = TWO_PI / points * (low_index[:, None] * high_index[None, :]).astype(jnp.float32)
    cosine = jnp.cos(twiddle)
    sine_part = jnp.sin(twiddle)
    rotated = jnp.stack(
        [
            section_one[0] * cosine + section_one[1] * sine_part,
            section_one[1] * cosine - section_one[0] * sine_part,
        ]
    ).astype(jnp.bfloat16)
    return jnp.einsum(
        "oimj,ispfkm->ospfkj", dft_table(CH_HI), rotated, preferred_element_type=jnp.float32
    ).astype(jnp.bfloat16)


def plain_weights(delays, beam_ids, groups, channel_low, station_total):
    points = CH_LO * CH_HI
    member = (groups[None, :] == (beam_ids % GROUPS)[:, None]).astype(jnp.float32)
    weight_scale = math.sqrt(GROUPS / station_total) * member
    channel = channel_low[:, None] + CH_LO * jnp.arange(CH_HI, dtype=jnp.int32)[None, :]
    fraction = channel.astype(jnp.float32) / float(points)
    phases = TWO_PI * (delays[:, :, None, None] * fraction[None, None])
    weight_re = (weight_scale[:, :, None, None] * jnp.cos(phases)).astype(jnp.bfloat16)
    weight_im = (-weight_scale[:, :, None, None] * jnp.sin(phases)).astype(jnp.bfloat16)
    return (weight_re, weight_im)


def form_beams(weight_re, weight_im, channels):
    real_in = channels[0]
    imag_in = channels[1]

    def contract(weights_part, data_part):
        return jnp.einsum(
            "bsxc,spfxc->bpfxc", weights_part, data_part, preferred_element_type=jnp.float32
        )

    real_out = contract(weight_re, real_in) - contract(weight_im, imag_in)
    imag_out = contract(weight_re, imag_in) + contract(weight_im, real_in)
    return jnp.stack([real_out, imag_out], axis=1)


def select_delays(delay_rows, pointing):
    directions = jnp.arange(delay_rows.shape[0], dtype=jnp.int32)
    onehot = (pointing[:, None] == directions[None, :]).astype(jnp.float32)
    return jnp.dot(
        onehot, delay_rows, precision=lax.Precision.HIGHEST, preferred_element_type=jnp.float32
    )


def with_history(frames_own):
    frame_count = frames_own.shape[3]
    needed = TAPS - 1
    pieces = []
    hop_count = (needed + frame_count - 1) // frame_count
    for hop_step in range(1, hop_count + 1):
        take_count = min(frame_count, needed - (hop_step - 1) * frame_count)
        portion = frames_own[:, :, :, frame_count - take_count :, :]
        pieces.append(passed_along(portion, "tf", hop_step))
    return jnp.concatenate(pieces[::-1] + [frames_own], axis=3)


def plain_body(voltages, delay_table, beam_pointing, station_group):
    planes, stations_here, pol_count, samples_here = voltages.shape
    points = CH_LO * CH_HI
    frame_count = samples_here // points
    frames_own = voltages.reshape(planes, stations_here, pol_count, frame_count, points)
    channels = channelize(with_history(frames_own), frame_count)
    station_total = station_group.shape[0]
    beam_total = beam_pointing.shape[0]
    regrouped = lax.all_to_all(channels, "stn", split_axis=4, concat_axis=1, tiled=True)
    low_count = regrouped.shape[4]
    channel_low = lax.axis_index("stn") * low_count + jnp.arange(low_count, dtype=jnp.int32)
    beam_ids = jnp.arange(beam_total, dtype=jnp.int32)
    delays_all = select_delays(delay_table, beam_pointing)
    weight_re, weight_im = plain_weights(
        delays_all, beam_ids, station_group, channel_low, station_total
    )
    formed = form_beams(weight_re, weight_im, regrouped).astype(jnp.bfloat16)
    result = lax.all_to_all(
        lax.all_to_all(formed, "stn", split_axis=0, concat_axis=4, tiled=True),
        "tf",
        split_axis=4,
        concat_axis=3,
        tiled=True,
    )
    return result


def solution(mesh):
    in_specs = (P(None, "stn", None, "tf"), P(), P(), P())
    out_specs = P("stn", None, None, None, "tf", None)

    def spread_over(body):
        return jax.shard_map(
            body, mesh=mesh, in_specs=in_specs, out_specs=out_specs, check_vma=False
        )

    if mesh.shape["tf"] == TF and mesh.shape["stn"] == STN:
        return spread_over(fast_body)
    return spread_over(plain_body)
```

```python
import functools
import math

import jax
import jax.numpy as jnp
import numpy as np
from jax import lax
from jax.experimental import pallas as pl
from jax.experimental.pallas import tpu as pltpu
from jax.sharding import PartitionSpec as P


TAPS = 16
CH_LO = 32
CH_HI = 128
GROUPS = 4
POINTS = CH_LO * CH_HI
TWO_PI = 2.0 * math.pi
BF = jnp.bfloat16
F32 = jnp.float32

LANES = 128
TF = 4
STN = 8
HALF = STN // 2
UNROLL = 8
ROUNDS = ((2, 3, 4, 5), (0, 1, 6, 7))


def offset_in(chosen, place):
    return place + 4 * (place // 2) if chosen else place + 2


PART = CH_HI // TF
LOW = CH_LO // TF
PER = 4
CHUNKS = 2


def filter_window(position):
    total_len = float(TAPS * POINTS)
    value = position.astype(F32)
    hann_taper = 0.5 - 0.5 * jnp.cos(TWO_PI / total_len * value)
    return jnp.sinc((value - 0.5 * total_len) / float(POINTS)) * hann_taper


def window_rows(part):
    shape = (TAPS, 2 * CH_LO, LANES)
    tap = lax.broadcasted_iota(jnp.int32, shape, 0)
    n2 = lax.broadcasted_iota(jnp.int32, shape, 1) // 2
    n1 = part * PART + lax.broadcasted_iota(jnp.int32, shape, 2) % PART
    return filter_window(tap * POINTS + n2 * CH_HI + n1)


def dft_pair(points):
    counter = np.arange(points)
    angles = TWO_PI / points * (counter[:, None] * counter[None, :] % points)
    factor = 1.0 / math.sqrt(points)
    return np.cos(angles) * factor, np.sin(angles) * factor


def first_table():
    cosine, sine = dft_pair(CH_LO)
    planes = np.stack([np.stack([cosine, sine]), np.stack([-sine, cosine])])
    planes = planes.reshape(2, 2, TF, LOW, CH_LO)
    table = np.einsum("oitkn,pr->otpkinr", planes, np.eye(2))
    return jnp.asarray(table.reshape(2, TF, 2 * LOW, 4 * CH_LO), BF)


def second_table():
    cosine, sine = dft_pair(CH_HI)
    table = np.block([[cosine, -sine], [sine, cosine]])
    return jnp.asarray(table.reshape(2, TF, PART, 2 * CH_HI), BF)


def twiddle_rows(part):
    shape = (TF, 2 * LOW, LANES)
    k2 = lax.broadcasted_iota(jnp.int32, shape, 0) * LOW
    k2 = k2 + lax.broadcasted_iota(jnp.int32, shape, 1) % LOW
    n1 = part * PART + lax.broadcasted_iota(jnp.int32, shape, 2) % PART
    angle = TWO_PI / POINTS * (k2 * n1).astype(F32)
    return jnp.cos(angle), jnp.sin(angle)


VMEM = pl.BlockSpec(memory_space=pltpu.VMEM)
SMEM = pl.BlockSpec(memory_space=pltpu.SMEM)
HBM = pl.BlockSpec(memory_space=pltpu.HBM)


def params(mib):
    return pltpu.CompilerParams(vmem_limit_bytes=mib << 20)


def cost(mib, flops=0):
    return pl.CostEstimate(flops=flops, bytes_accessed=mib << 20, transcendentals=0)


def swap_lane_blocks(parts):
    lane = lax.broadcasted_iota(jnp.int32, parts[0].shape, 1)
    upper = lane >= 2 * PART
    odd = (lane // PART) % 2 == 1
    turned = [pltpu.roll(part, 2 * PART, 1) for part in parts]
    half = [
        jnp.where(upper, turned[2], parts[0]),
        jnp.where(upper, turned[3], parts[1]),
        jnp.where(upper, parts[2], turned[0]),
        jnp.where(upper, parts[3], turned[1]),
    ]
    out = []
    for low, high in ((half[0], half[1]), (half[2], half[3])):
        out.append(jnp.where(odd, pltpu.roll(high, PART, 1), low))
        out.append(jnp.where(odd, high, pltpu.roll(low, LANES - PART, 1)))
    return out


def spread_kernel(chunk, me_ref, volt_ref, *refs):
    outs, (in_ref, sem) = refs[:TF], refs[TF:]
    planes, _, frames = volt_ref.shape[:3]
    half = frames // 2
    steps = [(q, part) for q in range(planes) for part in range(2)]
    reads = [
        pltpu.make_async_copy(
            volt_ref.at[q, pl.ds(chunk * PER, PER), pl.ds(part * half, half)],
            in_ref.at[q, :, pl.ds(part * half, half)],
            sem.at[q, part],
        )
        for q, part in steps
    ]
    for read in reads:
        read.start()
    for (q, part), read in zip(steps, reads):
        read.wait()
        for me in range(TF):

            @pl.when(me_ref[0] == me)
            def _(me=me, q=q, part=part):
                def one(f, carry):
                    parts = [in_ref[q, a, f] for a in range(PER)]
                    for j, block in enumerate(swap_lane_blocks(parts)):
                        outs[j ^ me][q, f] = block
                    return carry

                lax.fori_loop(part * half, (part + 1) * half, one, 0, unroll=2)


def spread(me, volt, chunk):
    planes, _, frames, rows, _ = volt.shape
    return pl.pallas_call(
        functools.partial(spread_kernel, chunk),
        name="spread",
        in_specs=[SMEM, HBM],
        out_specs=[VMEM] * TF,
        out_shape=[jax.ShapeDtypeStruct((planes, frames, rows, LANES), BF)] * TF,
        scratch_shapes=[
            pltpu.VMEM((planes, PER, frames, rows, LANES), BF),
            pltpu.SemaphoreType.DMA((planes, 2)),
        ],
        compiler_params=params(4),
        cost_estimate=cost(4),
    )(me, pltpu.with_memory_space_constraint(volt, pltpu.HBM))


def channel_kernel(split, at_ref, *refs):
    sources = refs[:TF]
    win_ref, table_ref, cos_ref, sin_ref = refs[TF : TF + 4]
    stage_ref, filt_ref = refs[-2:] if split else refs[-4:-2]
    me, owner = at_ref[0], at_ref[1]
    rows = 2 * CH_LO
    history = TAPS - 1
    planes, per_source = sources[0].shape[:2]
    frames = TF * per_source
    for d, ref in enumerate(sources):
        stage_ref[:, pl.ds((me ^ d) * per_source, per_source)] = ref[...]

    strip = 16

    def one_strip(q, step, carry):
        at = pl.multiple_of(step * strip, strip)
        data = [stage_ref[q, f, pl.ds(at, strip), :].astype(F32) for f in range(frames)]
        taps = [win_ref[tap, pl.ds(at, strip), :] for tap in range(TAPS)]
        for f in range(frames):
            total = None
            for tap in range(max(0, history - f), TAPS):
                term = taps[tap] * data[f + tap - history]
                total = term if total is None else total + term
            filt_ref[f, q, pl.ds(at, strip), :] = total.astype(BF)
        return carry

    for q in range(planes):
        lax.fori_loop(0, rows // strip, functools.partial(one_strip, q), 0)

    ranges = [(me ^ t) if split else t for t in range(TF)]
    table = jnp.concatenate([table_ref[o, t] for o in range(planes) for t in ranges], axis=0)
    per_dest = frames // STN
    if split:
        outs = refs[TF + 4 : TF + 4 + 2 * TF]
    else:
        out_ref, done_ref, sem = refs[TF + 4], refs[-2], refs[-1]

        def send(dest):
            return pltpu.make_async_copy(done_ref.at[dest], out_ref.at[dest], sem.at[dest])

    def one_dest(chosen, step, carry):
        dest = owner ^ offset_in(chosen, step) if split else step
        cosine = jnp.concatenate([cos_ref[t] for t in ranges], axis=0)
        sine = jnp.concatenate([sin_ref[t] for t in ranges], axis=0)
        for pair in range(per_dest // 2):
            f = per_dest * dest + 2 * pair
            left = filt_ref[f].reshape(2 * rows, LANES)
            right = filt_ref[f + 1].reshape(2 * rows, LANES)
            both = jnp.concatenate([left, right], axis=1)
            spectrum = jnp.dot(table, both, preferred_element_type=F32)
            for side in range(2):
                real = spectrum[:rows, side * LANES : (side + 1) * LANES]
                imag = spectrum[rows:, side * LANES : (side + 1) * LANES]
                turned = (real * cosine + imag * sine, imag * cosine - real * sine)
                for o in range(2):
                    value = turned[o].astype(BF).reshape(TF, 2 * LOW, LANES)
                    if split:
                        for d in range(TF):
                            outs[chosen * TF + d][step, o, 2 * pair + side] = value[d]
                    else:
                        done_ref[dest, :, o, 2 * pair + side] = value
        if not split:
            send(dest).start()
        return carry

    if split:
        for chosen in range(2):
            lax.fori_loop(0, HALF, functools.partial(one_dest, chosen), 0, unroll=2)
    else:
        lax.fori_loop(0, STN, functools.partial(one_dest, 0), 0, unroll=2)
        for dest in range(STN):
            send(dest).wait()


def channel_step(at, blocks, window, table, cosine, sine, split):
    planes, per_source, rows, _ = blocks[0].shape
    frames = TF * per_source
    tail = (planes, frames // STN, 2 * LOW, LANES)
    scratch = [
        pltpu.VMEM((planes, frames, rows, LANES), BF),
        pltpu.VMEM((frames, planes, rows, LANES), BF),
    ]
    if split:
        out_shape = [jax.ShapeDtypeStruct((HALF,) + tail, BF)] * (2 * TF)
        out_specs = [VMEM] * (2 * TF)
    else:
        out = (STN, TF) + tail
        out_shape, out_specs = jax.ShapeDtypeStruct(out, BF), HBM
        scratch += [pltpu.VMEM(out, BF), pltpu.SemaphoreType.DMA((STN,))]
    return pl.pallas_call(
        functools.partial(channel_kernel, split),
        name="channel_step",
        in_specs=[SMEM] + [VMEM] * (TF + 4),
        out_specs=out_specs,
        out_shape=out_shape,
        scratch_shapes=scratch,
        compiler_params=params(12),
        cost_estimate=cost(8, 1 << 29),
    )(at, *blocks, window, table, cosine, sine)


def turned_by(turns):
    quarter = jnp.round(4.0 * turns)
    angle = TWO_PI * (turns - 0.25 * quarter)
    square = angle * angle
    sine = angle * (
        1.0 + square * (-1.0 / 6 + square * (1.0 / 120 + square * (-1.0 / 5040 + square * (1.0 / 362880))))
    )
    cosine = 1.0 + square * (
        -0.5 + square * (1.0 / 24 + square * (-1.0 / 720 + square * (1.0 / 40320)))
    )
    turn = quarter.astype(jnp.int32) & 3
    odd = (turn & 1) == 1
    base_cos = jnp.where(odd, sine, cosine)
    base_sin = jnp.where(odd, cosine, sine)
    real = jnp.where((turn == 1) | (turn == 2), -base_cos, base_cos)
    return real, jnp.where(turn >= 2, -base_sin, base_sin)


def weight_kernel(chunk, offset_of, at_ref, table_ref, beam_ref, group_ref, out_ref, order_ref, count_ref, row_ref):
    total = group_ref.shape[0]
    members = out_ref.shape[0] - 1
    offsets = out_ref.shape[1]
    scale = math.sqrt(GROUPS / total)
    shape = (LOW, LANES)
    sublane = lax.broadcasted_iota(jnp.int32, shape, 0)
    lane = lax.broadcasted_iota(jnp.int32, shape, 1)
    high = (at_ref[0] * LOW + CH_LO * lane).astype(F32) / float(POINTS)
    low = sublane.astype(F32) / float(POINTS)
    for g in range(GROUPS):
        count_ref[g] = 0

    def some_members(step, carry):
        for slot in range(UNROLL):
            one_member(step * UNROLL + slot, slot)
        return carry

    def one_member(member, slot):
        source = offset_of(member // PER, at_ref[1])
        s = source * (PER * CHUNKS) + chunk * PER + member % PER
        group = group_ref[s]
        at = count_ref[group]
        order_ref[group, at] = member
        order_ref[group, at + 1] = members
        count_ref[group] = at + 1

        down = jnp.zeros(shape, F32)
        across = jnp.zeros(shape, F32)
        for d in range(offsets):
            beam = group + GROUPS * (at_ref[1] ^ d)
            delay = table_ref[beam_ref[beam], s]
            down = jnp.where(sublane == d, delay, down)
            across = jnp.where(lane == d, delay, across)
        real, imag = turned_by(down * high)
        row_ref[slot, 0] = scale * real
        row_ref[slot, 1] = -scale * imag
        real, imag = turned_by(across * low)
        imag = -imag
        for d in range(offsets):
            high_re = row_ref[slot, 0, pl.ds(d, 1), :]
            high_im = row_ref[slot, 1, pl.ds(d, 1), :]
            low_re = jnp.broadcast_to(real[:, d : d + 1], shape)
            low_im = jnp.broadcast_to(imag[:, d : d + 1], shape)
            out_ref[member, d, 0] = (high_re * low_re - high_im * low_im).astype(BF)
            out_ref[member, d, 1] = (high_re * low_im + high_im * low_re).astype(BF)

    out_ref[members] = jnp.zeros(out_ref.shape[1:], BF)
    lax.fori_loop(0, members // UNROLL, some_members, 0)


def beam_weights(at, chosen, delay_table, beam_pointing, station_group):
    chunk = 0 if chosen is None else 1
    members = (HALF if chunk else STN) * PER

    def offset_of(place, owner):
        return place if chosen is None else offset_in(chosen, place) ^ owner

    offsets = beam_pointing.shape[0] // GROUPS
    out = (members + 1, offsets, 2, LOW, LANES)
    return pl.pallas_call(
        functools.partial(weight_kernel, chunk, offset_of),
        name="beam_weights",
        in_specs=[SMEM] * 4,
        out_specs=[VMEM, SMEM, SMEM],
        out_shape=[
            jax.ShapeDtypeStruct(out, BF),
            jax.ShapeDtypeStruct((GROUPS, members + 2), jnp.int32),
            jax.ShapeDtypeStruct((GROUPS,), jnp.int32),
        ],
        scratch_shapes=[pltpu.VMEM((UNROLL, 2, LOW, LANES), F32)],
        compiler_params=params(8),
        cost_estimate=cost(8, 1 << 29),
    )(at, delay_table, beam_pointing, station_group)


def transform(parts_of, table, put):
    planes = [swap_lane_blocks(parts_of(o)) for o in range(2)]
    for a in range(PER):
        both = jnp.concatenate([planes[0][a], planes[1][a]], axis=1)
        spectrum = jnp.dot(both, table, preferred_element_type=F32)
        for o in range(2):
            put(a, o, spectrum[:, o * LANES : (o + 1) * LANES])


def table_of(table_ref, parts):
    return jnp.concatenate([table_ref[q, j] for q in range(2) for j in parts], axis=0)


def middle_kernel(at_ref, *refs):
    blocks, table_ref, outs = refs[:TF], refs[TF], refs[TF + 1 :]
    me = at_ref[0]
    per_dest = blocks[0].shape[2]
    table = table_of(table_ref, [me ^ d for d in range(TF)])
    for place, out in enumerate(outs):

        def parts_of(o, place=place):
            return [block[place, o].reshape(per_dest * 2 * LOW, LANES) for block in blocks]

        def put(a, o, value, out=out):
            out[a, o] = value.astype(BF)

        transform(parts_of, table, put)


def middle_step(at, blocks, table):
    _, planes, per_dest, _, _ = blocks[0].shape
    out = (PER, planes, per_dest * 2 * LOW, LANES)
    return pl.pallas_call(
        middle_kernel,
        name="middle_step",
        in_specs=[SMEM] + [VMEM] * (TF + 1),
        out_specs=[VMEM] * HALF,
        out_shape=[jax.ShapeDtypeStruct(out, BF)] * HALF,
        compiler_params=params(4),
        cost_estimate=cost(4, 1 << 28),
    )(at, *blocks, table)


def spread_weights(offsets, weight_ref, wide_ref):
    def one(member, carry):
        for i, d in enumerate(offsets):
            real, imag = weight_ref[member, d, 0].astype(F32), weight_ref[member, d, 1].astype(F32)
            wide_ref[member, i, 0] = real
            wide_ref[member, i, 1] = imag - real
            wide_ref[member, i, 2] = imag + real
        return carry

    lax.fori_loop(0, weight_ref.shape[0], one, 0, unroll=4)


def form_beams_of(offsets, chan_ref, wide_ref, order_ref, count_ref, put, ready=lambda g: None):
    count = len(offsets)
    wide = 16 // count
    blocks = chan_ref.shape[2] // wide

    def one_block(g, step, carry):
        base = step * wide

        def one_pair(pair, acc):
            acc = list(acc)
            for member in (order_ref[g, 2 * pair], order_ref[g, 2 * pair + 1]):
                data = []
                for x in range(wide):
                    re, im = chan_ref[member, 0, base + x], chan_ref[member, 1, base + x]
                    data.append((re + im, re, im))
                for i, d in enumerate(offsets):
                    for y in range(3):
                        weight = wide_ref[member, i, y]
                        for x in range(wide):
                            at = (i * 3 + y) * wide + x
                            acc[at] = acc[at] + weight * data[x][y]
            return tuple(acc)

        zero = jnp.zeros((LOW, LANES), F32)
        pairs = (count_ref[g] + 1) // 2
        acc = lax.fori_loop(0, pairs, one_pair, (zero,) * (3 * count * wide))
        for i, d in enumerate(offsets):
            for x in range(wide):
                both, re, im = (acc[(i * 3 + y) * wide + x] for y in range(3))
                put(d, g, 0, base + x, both - im)
                put(d, g, 1, base + x, both + re)
        return carry

    for g in range(GROUPS):
        ready(g)
        lax.fori_loop(0, blocks, functools.partial(one_block, g), 0)


def early_kernel(blocks_ref, table_ref, weight_ref, order_ref, count_ref, sum_hbm, chan_ref, sum_ref, wide_ref, sem):
    offsets = range(weight_ref.shape[1])
    spread_weights(offsets, weight_ref, wide_ref)
    sources, _, _, per_dest = blocks_ref.shape[:4]
    table = table_of(table_ref, range(TF))
    for src in range(sources):

        def parts_of(o, src=src):
            return [blocks_ref[src, j, o].reshape(per_dest * 2 * LOW, LANES) for j in range(TF)]

        def put(a, o, value, src=src):
            chan_ref[src * PER + a, o] = value.reshape(per_dest * 2, LOW, LANES)

        transform(parts_of, table, put)
    chan_ref[chan_ref.shape[0] - 1] = jnp.zeros(chan_ref.shape[1:], F32)


    def keep(d, g, o, fp, value):
        sum_ref[d, g, o, fp % 2, fp // 2] = value

    form_beams_of(offsets, chan_ref, wide_ref, order_ref, count_ref, keep)
    write = pltpu.make_async_copy(sum_ref, sum_hbm, sem)
    write.start()
    write.wait()


def late_kernel(last, weight_ref, order_ref, count_ref, sum_hbm, *refs):
    sum_ref, wide_ref, chan_ref, sem = refs[-4:]
    sources = chan_ref.shape[0] // PER
    blocks, outs = refs[:sources], refs[sources:-4]
    reads = [
        pltpu.make_async_copy(sum_hbm.at[:, g], sum_ref.at[:, g], sem.at[g]) for g in range(GROUPS)
    ]
    for read in reads:
        read.start()
    offsets = range(weight_ref.shape[1])
    spread_weights(offsets, weight_ref, wide_ref)
    members, planes, both = chan_ref.shape[:3]
    for place, block in enumerate(blocks):
        value = block[...].astype(F32)
        chan_ref[pl.ds(place * PER, PER)] = value.reshape(PER, planes, both, LOW, LANES)
    chan_ref[members - 1] = jnp.zeros(chan_ref.shape[1:], F32)

    def ready(g):
        reads[g].wait()

    def put(d, g, o, fp, value):
        f, p = fp // 2, fp % 2
        value = value + sum_ref[d, g, o, p, f]
        if last:
            outs[d][g, o, p, f] = value.astype(BF)
        else:
            sum_ref[d, g, o, p, f] = value

    form_beams_of(offsets, chan_ref, wide_ref, order_ref, count_ref, put, ready)
    if not last:
        write = pltpu.make_async_copy(sum_ref, outs[0], sem.at[0])
        write.start()
        write.wait()


def beams_early(blocks, table, weights, order, count):
    planes, per_dest = blocks.shape[2:4]
    out = (weights.shape[1], GROUPS, planes, 2, per_dest, LOW, LANES)
    return pl.pallas_call(
        early_kernel,
        name="beams_early",
        in_specs=[VMEM] * 3 + [SMEM] * 2,
        out_specs=HBM,
        out_shape=jax.ShapeDtypeStruct(out, F32),
        scratch_shapes=[
            pltpu.VMEM((weights.shape[0], planes, 2 * per_dest, LOW, LANES), F32),
            pltpu.VMEM(out, F32),
            pltpu.VMEM(weights.shape[:2] + (3, LOW, LANES), F32),
            pltpu.SemaphoreType.DMA,
        ],
        compiler_params=params(12),
        cost_estimate=cost(8, 1 << 29),
    )(blocks, table, weights, order, count)


def beams_late(last, blocks, weights, order, count, partial):
    one = partial.shape[1:]
    members = weights.shape[0]
    if last:
        out_shape, out_specs = [jax.ShapeDtypeStruct(one, BF)] * partial.shape[0], [VMEM] * partial.shape[0]
    else:
        out_shape, out_specs = jax.ShapeDtypeStruct(partial.shape, F32), HBM
    return pl.pallas_call(
        functools.partial(late_kernel, last),
        name="beams_late",
        in_specs=[VMEM, SMEM, SMEM, HBM] + [VMEM] * len(blocks),
        out_specs=out_specs,
        out_shape=out_shape,
        scratch_shapes=[
            pltpu.VMEM(partial.shape, F32),
            pltpu.VMEM((members, partial.shape[0], 3, LOW, LANES), F32),
            pltpu.VMEM((members, one[1], one[2] * one[3], LOW, LANES), F32),
            pltpu.SemaphoreType.DMA((GROUPS,)),
        ],
        compiler_params=params(12),
        cost_estimate=cost(8, 1 << 29),
    )(weights, order, count, partial, *blocks)


def gather_kernel(me_ref, *refs):
    parts, out_ref, sem = refs[:STN], refs[STN], refs[STN + 1]
    per_dest = parts[0].shape[3]
    copies = []
    for d, part in enumerate(parts):
        frames = pl.ds((me_ref[0] ^ d) * per_dest, per_dest)
        copies.append(pltpu.make_async_copy(part, out_ref.at[:, :, :, frames], sem.at[d]))
    for copy in copies:
        copy.start()
    for copy in copies:
        copy.wait()


def gather_frames(me, parts):
    shape = parts[0].shape
    shape = shape[:3] + (shape[3] * len(parts),) + shape[4:]
    return pl.pallas_call(
        gather_kernel,
        name="gather_frames",
        in_specs=[SMEM] + [VMEM] * len(parts),
        out_specs=pl.BlockSpec(memory_space=pl.ANY),
        out_shape=jax.ShapeDtypeStruct(shape, BF),
        scratch_shapes=[pltpu.SemaphoreType.DMA((len(parts),))],
        compiler_params=params(4),
    )(me, *parts)


def swapped(value, axis, offset):
    count = lax.axis_size(axis)
    return lax.ppermute(value, axis, [(i, i ^ offset) for i in range(count)])


def fast_body(voltages, delay_table, beam_pointing, station_group):
    planes, stations_here, pols, samples_here = voltages.shape
    part, home = lax.axis_index("tf"), lax.axis_index("stn")
    me = part.astype(jnp.int32).reshape(1)
    owner = home.astype(jnp.int32).reshape(1)
    at = jnp.concatenate([me, owner])
    rows = samples_here // LANES
    volt = voltages.reshape(planes, stations_here, pols, rows, LANES)
    volt = volt.transpose(0, 1, 3, 2, 4)
    volt = volt.reshape(planes, stations_here, rows // CH_LO, CH_LO * pols, LANES)
    cosine, sine = twiddle_rows(part)
    window, first, second = window_rows(part), first_table(), second_table()

    blocks = []
    for chunk in range(CHUNKS):
        own = spread(me, volt, chunk)
        row = [own[0]]
        for d in range(1, TF):
            row.append(swapped(own[d], "tf", d))
        blocks.append(row)

    value = channel_step(at, blocks[0], window, first, cosine, sine, False)
    shape = value.shape
    value = value.reshape((STN * TF,) + shape[2:])
    value = lax.all_to_all(value, ("stn", "tf"), split_axis=0, concat_axis=0, tiled=True)
    turned = value.reshape(shape)

    own = channel_step(at, blocks[1], window, first, cosine, sine, True)
    late = [None] * STN
    for chosen, offsets in enumerate(ROUNDS):
        row = [own[chosen * TF]]
        for d in range(1, TF):
            row.append(swapped(own[chosen * TF + d], "tf", d))
        sent = middle_step(at, row, second)
        for e, value in zip(offsets, sent):
            late[e] = swapped(value, "stn", e) if e else value

    args = (delay_table, beam_pointing, station_group)
    weights = beam_weights(at, None, *args)
    partial = beams_early(turned, second, *weights)
    weights = beam_weights(at, 0, *args)
    partial = beams_late(False, [late[e] for e in ROUNDS[0]], *weights, partial)
    weights = beam_weights(at, 1, *args)
    parts = list(beams_late(True, [late[e] for e in ROUNDS[1]], *weights, partial))
    for d in range(1, STN):
        parts[d] = swapped(parts[d], "stn", d)
    return gather_frames(owner, parts)


def passed_along(value, axis, steps):
    count = lax.axis_size(axis)
    first, last = (max(0, -steps), min(count, count - steps))
    return lax.ppermute(value, axis, [(source, source + steps) for source in range(first, last)])


def plain_window(tap_count, points):
    position = jnp.arange(tap_count * points, dtype=jnp.int32).astype(jnp.float32)
    total_len = float(tap_count * points)
    hann_taper = 0.5 - 0.5 * jnp.cos(TWO_PI / total_len * position)
    kernel = jnp.sinc((position - 0.5 * total_len) / float(points)) * hann_taper
    return kernel.reshape(tap_count, points)


def dft_table(points):
    counter = jnp.arange(points, dtype=jnp.int32)
    product = counter[:, None] * counter[None, :] % points
    angles = TWO_PI / points * product.astype(jnp.float32)
    factor = 1.0 / math.sqrt(points)
    cosine = jnp.cos(angles) * factor
    sine_part = jnp.sin(angles) * factor
    stacked = jnp.stack([jnp.stack([cosine, sine_part]), jnp.stack([-sine_part, cosine])])
    return stacked.astype(jnp.bfloat16)


def channelize(extended, frame_count):
    points = CH_LO * CH_HI
    window = plain_window(TAPS, points)
    filtered = sum(
        (
            window[tap_step]
            * extended[:, :, :, tap_step : tap_step + frame_count, :].astype(jnp.float32)
            for tap_step in range(TAPS)
        )
    )
    filtered = filtered.astype(jnp.bfloat16)
    shaped = filtered.reshape(filtered.shape[:4] + (CH_LO, CH_HI))
    section_one = jnp.einsum(
        "oikn,ispfnm->ospfkm", dft_table(CH_LO), shaped, preferred_element_type=jnp.float32
    )
    low_index = jnp.arange(CH_LO, dtype=jnp.int32)
    high_index = jnp.arange(CH_HI, dtype=jnp.int32)
    twiddle = TWO_PI / points * (low_index[:, None] * high_index[None, :]).astype(jnp.float32)
    cosine = jnp.cos(twiddle)
    sine_part = jnp.sin(twiddle)
    rotated = jnp.stack(
        [
            section_one[0] * cosine + section_one[1] * sine_part,
            section_one[1] * cosine - section_one[0] * sine_part,
        ]
    ).astype(jnp.bfloat16)
    return jnp.einsum(
        "oimj,ispfkm->ospfkj", dft_table(CH_HI), rotated, preferred_element_type=jnp.float32
    ).astype(jnp.bfloat16)


def plain_weights(delays, beam_ids, groups, channel_low, station_total):
    points = CH_LO * CH_HI
    member = (groups[None, :] == (beam_ids % GROUPS)[:, None]).astype(jnp.float32)
    weight_scale = math.sqrt(GROUPS / station_total) * member
    channel = channel_low[:, None] + CH_LO * jnp.arange(CH_HI, dtype=jnp.int32)[None, :]
    fraction = channel.astype(jnp.float32) / float(points)
    phases = TWO_PI * (delays[:, :, None, None] * fraction[None, None])
    weight_re = (weight_scale[:, :, None, None] * jnp.cos(phases)).astype(jnp.bfloat16)
    weight_im = (-weight_scale[:, :, None, None] * jnp.sin(phases)).astype(jnp.bfloat16)
    return (weight_re, weight_im)


def form_beams(weight_re, weight_im, channels):
    real_in = channels[0]
    imag_in = channels[1]

    def contract(weights_part, data_part):
        return jnp.einsum(
            "bsxc,spfxc->bpfxc", weights_part, data_part, preferred_element_type=jnp.float32
        )

    real_out = contract(weight_re, real_in) - contract(weight_im, imag_in)
    imag_out = contract(weight_re, imag_in) + contract(weight_im, real_in)
    return jnp.stack([real_out, imag_out], axis=1)


def select_delays(delay_rows, pointing):
    directions = jnp.arange(delay_rows.shape[0], dtype=jnp.int32)
    onehot = (pointing[:, None] == directions[None, :]).astype(jnp.float32)
    return jnp.dot(
        onehot, delay_rows, precision=lax.Precision.HIGHEST, preferred_element_type=jnp.float32
    )


def with_history(frames_own):
    frame_count = frames_own.shape[3]
    needed = TAPS - 1
    pieces = []
    hop_count = (needed + frame_count - 1) // frame_count
    for hop_step in range(1, hop_count + 1):
        take_count = min(frame_count, needed - (hop_step - 1) * frame_count)
        portion = frames_own[:, :, :, frame_count - take_count :, :]
        pieces.append(passed_along(portion, "tf", hop_step))
    return jnp.concatenate(pieces[::-1] + [frames_own], axis=3)


def plain_body(voltages, delay_table, beam_pointing, station_group):
    planes, stations_here, pol_count, samples_here = voltages.shape
    points = CH_LO * CH_HI
    frame_count = samples_here // points
    frames_own = voltages.reshape(planes, stations_here, pol_count, frame_count, points)
    channels = channelize(with_history(frames_own), frame_count)
    station_total = station_group.shape[0]
    beam_total = beam_pointing.shape[0]
    regrouped = lax.all_to_all(channels, "stn", split_axis=4, concat_axis=1, tiled=True)
    low_count = regrouped.shape[4]
    channel_low = lax.axis_index("stn") * low_count + jnp.arange(low_count, dtype=jnp.int32)
    beam_ids = jnp.arange(beam_total, dtype=jnp.int32)
    delays_all = select_delays(delay_table, beam_pointing)
    weight_re, weight_im = plain_weights(
        delays_all, beam_ids, station_group, channel_low, station_total
    )
    formed = form_beams(weight_re, weight_im, regrouped).astype(jnp.bfloat16)
    result = lax.all_to_all(
        lax.all_to_all(formed, "stn", split_axis=0, concat_axis=4, tiled=True),
        "tf",
        split_axis=4,
        concat_axis=3,
        tiled=True,
    )
    return result


def solution(mesh):
    in_specs = (P(None, "stn", None, "tf"), P(), P(), P())
    out_specs = P("stn", None, None, None, "tf", None)

    def spread_over(body):
        return jax.shard_map(
            body, mesh=mesh, in_specs=in_specs, out_specs=out_specs, check_vma=False
        )

    if mesh.shape["tf"] == TF and mesh.shape["stn"] == STN:
        return spread_over(fast_body)
    return spread_over(plain_body)
```

```python
import functools
import math

import jax
import jax.numpy as jnp
import numpy as np
from jax import lax
from jax.experimental import pallas as pl
from jax.experimental.pallas import tpu as pltpu
from jax.sharding import PartitionSpec as P


TAPS = 16
CH_LO = 32
CH_HI = 128
GROUPS = 4
POINTS = CH_LO * CH_HI
TWO_PI = 2.0 * math.pi
BF = jnp.bfloat16
F32 = jnp.float32

LANES = 128
TF = 4
STN = 8
HALF = STN // 2
UNROLL = 8
ROUNDS = ((2, 3, 4, 5), (0, 1, 6, 7))


def offset_in(chosen, place):
    return place + 4 * (place // 2) if chosen else place + 2


PART = CH_HI // TF
LOW = CH_LO // TF
PER = 4
CHUNKS = 2


def filter_window(position):
    total_len = float(TAPS * POINTS)
    value = position.astype(F32)
    hann_taper = 0.5 - 0.5 * jnp.cos(TWO_PI / total_len * value)
    return jnp.sinc((value - 0.5 * total_len) / float(POINTS)) * hann_taper


def window_rows(part):
    shape = (TAPS, 2 * CH_LO, LANES)
    tap = lax.broadcasted_iota(jnp.int32, shape, 0)
    n2 = lax.broadcasted_iota(jnp.int32, shape, 1) // 2
    n1 = part * PART + lax.broadcasted_iota(jnp.int32, shape, 2) % PART
    return filter_window(tap * POINTS + n2 * CH_HI + n1)


def dft_pair(points):
    counter = np.arange(points)
    angles = TWO_PI / points * (counter[:, None] * counter[None, :] % points)
    factor = 1.0 / math.sqrt(points)
    return np.cos(angles) * factor, np.sin(angles) * factor


def first_table():
    cosine, sine = dft_pair(CH_LO)
    planes = np.stack([np.stack([cosine, sine]), np.stack([-sine, cosine])])
    planes = planes.reshape(2, 2, TF, LOW, CH_LO)
    table = np.einsum("oitkn,pr->otpkinr", planes, np.eye(2))
    return jnp.asarray(table.reshape(2, TF, 2 * LOW, 4 * CH_LO), BF)


def second_table():
    cosine, sine = dft_pair(CH_HI)
    table = np.block([[cosine, -sine], [sine, cosine]])
    return jnp.asarray(table.reshape(2, TF, PART, 2 * CH_HI), BF)


def twiddle_rows(part):
    shape = (TF, 2 * LOW, LANES)
    k2 = lax.broadcasted_iota(jnp.int32, shape, 0) * LOW
    k2 = k2 + lax.broadcasted_iota(jnp.int32, shape, 1) % LOW
    n1 = part * PART + lax.broadcasted_iota(jnp.int32, shape, 2) % PART
    angle = TWO_PI / POINTS * (k2 * n1).astype(F32)
    return jnp.cos(angle), jnp.sin(angle)


VMEM = pl.BlockSpec(memory_space=pltpu.VMEM)
SMEM = pl.BlockSpec(memory_space=pltpu.SMEM)
HBM = pl.BlockSpec(memory_space=pltpu.HBM)


def params(mib):
    return pltpu.CompilerParams(vmem_limit_bytes=mib << 20)


def cost(mib, flops=0):
    return pl.CostEstimate(flops=flops, bytes_accessed=mib << 20, transcendentals=0)


def swap_lane_blocks(parts):
    lane = lax.broadcasted_iota(jnp.int32, parts[0].shape, 1)
    upper = lane >= 2 * PART
    odd = (lane // PART) % 2 == 1
    turned = [pltpu.roll(part, 2 * PART, 1) for part in parts]
    half = [
        jnp.where(upper, turned[2], parts[0]),
        jnp.where(upper, turned[3], parts[1]),
        jnp.where(upper, parts[2], turned[0]),
        jnp.where(upper, parts[3], turned[1]),
    ]
    out = []
    for low, high in ((half[0], half[1]), (half[2], half[3])):
        out.append(jnp.where(odd, pltpu.roll(high, PART, 1), low))
        out.append(jnp.where(odd, high, pltpu.roll(low, LANES - PART, 1)))
    return out


def spread_kernel(chunk, me_ref, volt_ref, *refs):
    outs, (in_ref, sem) = refs[:TF], refs[TF:]
    planes, _, frames = volt_ref.shape[:3]
    half = frames // 2
    steps = [(q, part) for q in range(planes) for part in range(2)]
    reads = [
        pltpu.make_async_copy(
            volt_ref.at[q, pl.ds(chunk * PER, PER), pl.ds(part * half, half)],
            in_ref.at[q, :, pl.ds(part * half, half)],
            sem.at[q, part],
        )
        for q, part in steps
    ]
    for read in reads:
        read.start()
    for (q, part), read in zip(steps, reads):
        read.wait()
        for me in range(TF):

            @pl.when(me_ref[0] == me)
            def _(me=me, q=q, part=part):
                def one(f, carry):
                    parts = [in_ref[q, a, f] for a in range(PER)]
                    for j, block in enumerate(swap_lane_blocks(parts)):
                        outs[j ^ me][q, f] = block
                    return carry

                lax.fori_loop(part * half, (part + 1) * half, one, 0, unroll=2)


def spread(me, volt, chunk):
    planes, _, frames, rows, _ = volt.shape
    return pl.pallas_call(
        functools.partial(spread_kernel, chunk),
        name="spread",
        in_specs=[SMEM, HBM],
        out_specs=[VMEM] * TF,
        out_shape=[jax.ShapeDtypeStruct((planes, frames, rows, LANES), BF)] * TF,
        scratch_shapes=[
            pltpu.VMEM((planes, PER, frames, rows, LANES), BF),
            pltpu.SemaphoreType.DMA((planes, 2)),
        ],
        compiler_params=params(4),
        cost_estimate=cost(4),
    )(me, pltpu.with_memory_space_constraint(volt, pltpu.HBM))


def channel_kernel(split, at_ref, *refs):
    sources = refs[:TF]
    win_ref, table_ref, cos_ref, sin_ref = refs[TF : TF + 4]
    stage_ref, filt_ref = refs[-2:] if split else refs[-4:-2]
    me, owner = at_ref[0], at_ref[1]
    rows = 2 * CH_LO
    history = TAPS - 1
    planes, per_source = sources[0].shape[:2]
    frames = TF * per_source
    for d, ref in enumerate(sources):
        stage_ref[:, pl.ds((me ^ d) * per_source, per_source)] = ref[...]

    strip = 16

    def one_strip(q, step, carry):
        at = pl.multiple_of(step * strip, strip)
        data = [stage_ref[q, f, pl.ds(at, strip), :].astype(F32) for f in range(frames)]
        taps = [win_ref[tap, pl.ds(at, strip), :] for tap in range(TAPS)]
        for f in range(frames):
            total = None
            for tap in range(max(0, history - f), TAPS):
                term = taps[tap] * data[f + tap - history]
                total = term if total is None else total + term
            filt_ref[f, q, pl.ds(at, strip), :] = total.astype(BF)
        return carry

    for q in range(planes):
        lax.fori_loop(0, rows // strip, functools.partial(one_strip, q), 0)

    ranges = [(me ^ t) if split else t for t in range(TF)]
    table = jnp.concatenate([table_ref[o, t] for o in range(planes) for t in ranges], axis=0)
    per_dest = frames // STN
    if split:
        outs = refs[TF + 4 : TF + 4 + 2 * TF]
    else:
        out_ref, done_ref, sem = refs[TF + 4], refs[-2], refs[-1]

        def send(dest):
            return pltpu.make_async_copy(done_ref.at[dest], out_ref.at[dest], sem.at[dest])

    def one_dest(chosen, step, carry):
        dest = owner ^ offset_in(chosen, step) if split else step
        cosine = jnp.concatenate([cos_ref[t] for t in ranges], axis=0)
        sine = jnp.concatenate([sin_ref[t] for t in ranges], axis=0)
        for pair in range(per_dest // 2):
            f = per_dest * dest + 2 * pair
            left = filt_ref[f].reshape(2 * rows, LANES)
            right = filt_ref[f + 1].reshape(2 * rows, LANES)
            both = jnp.concatenate([left, right], axis=1)
            spectrum = jnp.dot(table, both, preferred_element_type=F32)
            for side in range(2):
                real = spectrum[:rows, side * LANES : (side + 1) * LANES]
                imag = spectrum[rows:, side * LANES : (side + 1) * LANES]
                turned = (real * cosine + imag * sine, imag * cosine - real * sine)
                for o in range(2):
                    value = turned[o].astype(BF).reshape(TF, 2 * LOW, LANES)
                    if split:
                        for d in range(TF):
                            outs[chosen * TF + d][step, o, 2 * pair + side] = value[d]
                    else:
                        done_ref[dest, :, o, 2 * pair + side] = value
        if not split:
            send(dest).start()
        return carry

    if split:
        for chosen in range(2):
            lax.fori_loop(0, HALF, functools.partial(one_dest, chosen), 0, unroll=2)
    else:
        lax.fori_loop(0, STN, functools.partial(one_dest, 0), 0, unroll=2)
        for dest in range(STN):
            send(dest).wait()


def channel_step(at, blocks, window, table, cosine, sine, split):
    planes, per_source, rows, _ = blocks[0].shape
    frames = TF * per_source
    tail = (planes, frames // STN, 2 * LOW, LANES)
    scratch = [
        pltpu.VMEM((planes, frames, rows, LANES), BF),
        pltpu.VMEM((frames, planes, rows, LANES), BF),
    ]
    if split:
        out_shape = [jax.ShapeDtypeStruct((HALF,) + tail, BF)] * (2 * TF)
        out_specs = [VMEM] * (2 * TF)
    else:
        out = (STN, TF) + tail
        out_shape, out_specs = jax.ShapeDtypeStruct(out, BF), HBM
        scratch += [pltpu.VMEM(out, BF), pltpu.SemaphoreType.DMA((STN,))]
    return pl.pallas_call(
        functools.partial(channel_kernel, split),
        name="channel_step",
        in_specs=[SMEM] + [VMEM] * (TF + 4),
        out_specs=out_specs,
        out_shape=out_shape,
        scratch_shapes=scratch,
        compiler_params=params(12),
        cost_estimate=cost(8, 1 << 29),
    )(at, *blocks, window, table, cosine, sine)


def turned_by(turns):
    quarter = jnp.round(4.0 * turns)
    angle = TWO_PI * (turns - 0.25 * quarter)
    square = angle * angle
    sine = angle * (
        1.0 + square * (-1.0 / 6 + square * (1.0 / 120 + square * (-1.0 / 5040 + square * (1.0 / 362880))))
    )
    cosine = 1.0 + square * (
        -0.5 + square * (1.0 / 24 + square * (-1.0 / 720 + square * (1.0 / 40320)))
    )
    turn = quarter.astype(jnp.int32) & 3
    odd = (turn & 1) == 1
    base_cos = jnp.where(odd, sine, cosine)
    base_sin = jnp.where(odd, cosine, sine)
    real = jnp.where((turn == 1) | (turn == 2), -base_cos, base_cos)
    return real, jnp.where(turn >= 2, -base_sin, base_sin)


def weight_kernel(chunk, offset_of, at_ref, table_ref, beam_ref, group_ref, out_ref, order_ref, count_ref, row_ref):
    total = group_ref.shape[0]
    members = out_ref.shape[0] - 1
    offsets = out_ref.shape[1]
    scale = math.sqrt(GROUPS / total)
    shape = (LOW, LANES)
    sublane = lax.broadcasted_iota(jnp.int32, shape, 0)
    lane = lax.broadcasted_iota(jnp.int32, shape, 1)
    high = (at_ref[0] * LOW + CH_LO * lane).astype(F32) / float(POINTS)
    low = sublane.astype(F32) / float(POINTS)
    for g in range(GROUPS):
        count_ref[g] = 0

    def some_members(step, carry):
        for slot in range(UNROLL):
            one_member(step * UNROLL + slot, slot)
        return carry

    def one_member(member, slot):
        source = offset_of(member // PER, at_ref[1])
        s = source * (PER * CHUNKS) + chunk * PER + member % PER
        group = group_ref[s]
        at = count_ref[group]
        order_ref[group, at] = member
        order_ref[group, at + 1] = members
        count_ref[group] = at + 1

        down = jnp.zeros(shape, F32)
        across = jnp.zeros(shape, F32)
        for d in range(offsets):
            beam = group + GROUPS * (at_ref[1] ^ d)
            delay = table_ref[beam_ref[beam], s]
            down = jnp.where(sublane == d, delay, down)
            across = jnp.where(lane == d, delay, across)
        real, imag = turned_by(down * high)
        row_ref[slot, 0] = scale * real
        row_ref[slot, 1] = -scale * imag
        real, imag = turned_by(across * low)
        imag = -imag
        for d in range(offsets):
            high_re = row_ref[slot, 0, pl.ds(d, 1), :]
            high_im = row_ref[slot, 1, pl.ds(d, 1), :]
            low_re = jnp.broadcast_to(real[:, d : d + 1], shape)
            low_im = jnp.broadcast_to(imag[:, d : d + 1], shape)
            out_ref[member, d, 0] = (high_re * low_re - high_im * low_im).astype(BF)
            out_ref[member, d, 1] = (high_re * low_im + high_im * low_re).astype(BF)

    out_ref[members] = jnp.zeros(out_ref.shape[1:], BF)
    lax.fori_loop(0, members // UNROLL, some_members, 0)


def beam_weights(at, chosen, delay_table, beam_pointing, station_group):
    chunk = 0 if chosen is None else 1
    members = (HALF if chunk else STN) * PER

    def offset_of(place, owner):
        return place if chosen is None else (chosen * HALF + place) ^ owner

    offsets = beam_pointing.shape[0] // GROUPS
    out = (members + 1, offsets, 2, LOW, LANES)
    return pl.pallas_call(
        functools.partial(weight_kernel, chunk, offset_of),
        name="beam_weights",
        in_specs=[SMEM] * 4,
        out_specs=[VMEM, SMEM, SMEM],
        out_shape=[
            jax.ShapeDtypeStruct(out, BF),
            jax.ShapeDtypeStruct((GROUPS, members + 2), jnp.int32),
            jax.ShapeDtypeStruct((GROUPS,), jnp.int32),
        ],
        scratch_shapes=[pltpu.VMEM((UNROLL, 2, LOW, LANES), F32)],
        compiler_params=params(8),
        cost_estimate=cost(8, 1 << 29),
    )(at, delay_table, beam_pointing, station_group)


def transform(parts_of, table, put):
    planes = [swap_lane_blocks(parts_of(o)) for o in range(2)]
    for a in range(PER):
        both = jnp.concatenate([planes[0][a], planes[1][a]], axis=1)
        spectrum = jnp.dot(both, table, preferred_element_type=F32)
        for o in range(2):
            put(a, o, spectrum[:, o * LANES : (o + 1) * LANES])


def table_of(table_ref, parts):
    return jnp.concatenate([table_ref[q, j] for q in range(2) for j in parts], axis=0)


def middle_kernel(at_ref, *refs):
    blocks, table_ref, outs = refs[:TF], refs[TF], refs[TF + 1 :]
    me = at_ref[0]
    per_dest = blocks[0].shape[2]
    table = table_of(table_ref, [me ^ d for d in range(TF)])
    for place, out in enumerate(outs):

        def parts_of(o, place=place):
            return [block[place, o].reshape(per_dest * 2 * LOW, LANES) for block in blocks]

        def put(a, o, value, out=out):
            out[a, o] = value.astype(BF)

        transform(parts_of, table, put)


def middle_step(at, blocks, table):
    _, planes, per_dest, _, _ = blocks[0].shape
    out = (PER, planes, per_dest * 2 * LOW, LANES)
    return pl.pallas_call(
        middle_kernel,
        name="middle_step",
        in_specs=[SMEM] + [VMEM] * (TF + 1),
        out_specs=[VMEM] * HALF,
        out_shape=[jax.ShapeDtypeStruct(out, BF)] * HALF,
        compiler_params=params(4),
        cost_estimate=cost(4, 1 << 28),
    )(at, *blocks, table)


def spread_weights(offsets, weight_ref, wide_ref):
    def one(member, carry):
        for i, d in enumerate(offsets):
            real, imag = weight_ref[member, d, 0].astype(F32), weight_ref[member, d, 1].astype(F32)
            wide_ref[member, i, 0] = real
            wide_ref[member, i, 1] = imag - real
            wide_ref[member, i, 2] = imag + real
        return carry

    lax.fori_loop(0, weight_ref.shape[0], one, 0, unroll=4)


def form_beams_of(offsets, chan_ref, wide_ref, order_ref, count_ref, put, ready=lambda g: None):
    count = len(offsets)
    wide = 16 // count
    blocks = chan_ref.shape[2] // wide

    def one_block(g, step, carry):
        base = step * wide

        def one_pair(pair, acc):
            acc = list(acc)
            for member in (order_ref[g, 2 * pair], order_ref[g, 2 * pair + 1]):
                data = []
                for x in range(wide):
                    re, im = chan_ref[member, 0, base + x], chan_ref[member, 1, base + x]
                    data.append((re + im, re, im))
                for i, d in enumerate(offsets):
                    for y in range(3):
                        weight = wide_ref[member, i, y]
                        for x in range(wide):
                            at = (i * 3 + y) * wide + x
                            acc[at] = acc[at] + weight * data[x][y]
            return tuple(acc)

        zero = jnp.zeros((LOW, LANES), F32)
        pairs = (count_ref[g] + 1) // 2
        acc = lax.fori_loop(0, pairs, one_pair, (zero,) * (3 * count * wide))
        for i, d in enumerate(offsets):
            for x in range(wide):
                both, re, im = (acc[(i * 3 + y) * wide + x] for y in range(3))
                put(d, g, 0, base + x, both - im)
                put(d, g, 1, base + x, both + re)
        return carry

    for g in range(GROUPS):
        ready(g)
        lax.fori_loop(0, blocks, functools.partial(one_block, g), 0)


def early_kernel(blocks_ref, table_ref, weight_ref, order_ref, count_ref, sum_hbm, chan_ref, sum_ref, wide_ref, sem):
    offsets = range(weight_ref.shape[1])
    spread_weights(offsets, weight_ref, wide_ref)
    sources, _, _, per_dest = blocks_ref.shape[:4]
    table = table_of(table_ref, range(TF))
    for src in range(sources):

        def parts_of(o, src=src):
            return [blocks_ref[src, j, o].reshape(per_dest * 2 * LOW, LANES) for j in range(TF)]

        def put(a, o, value, src=src):
            chan_ref[src * PER + a, o] = value.reshape(per_dest * 2, LOW, LANES)

        transform(parts_of, table, put)
    chan_ref[chan_ref.shape[0] - 1] = jnp.zeros(chan_ref.shape[1:], F32)


    def keep(d, g, o, fp, value):
        sum_ref[d, g, o, fp % 2, fp // 2] = value

    form_beams_of(offsets, chan_ref, wide_ref, order_ref, count_ref, keep)
    write = pltpu.make_async_copy(sum_ref, sum_hbm, sem)
    write.start()
    write.wait()


def late_kernel(last, weight_ref, order_ref, count_ref, sum_hbm, *refs):
    sum_ref, wide_ref, chan_ref, sem = refs[-4:]
    sources = chan_ref.shape[0] // PER
    blocks, outs = refs[:sources], refs[sources:-4]
    reads = [
        pltpu.make_async_copy(sum_hbm.at[:, g], sum_ref.at[:, g], sem.at[g]) for g in range(GROUPS)
    ]
    for read in reads:
        read.start()
    offsets = range(weight_ref.shape[1])
    spread_weights(offsets, weight_ref, wide_ref)
    members, planes, both = chan_ref.shape[:3]
    for place, block in enumerate(blocks):
        value = block[...].astype(F32)
        chan_ref[pl.ds(place * PER, PER)] = value.reshape(PER, planes, both, LOW, LANES)
    chan_ref[members - 1] = jnp.zeros(chan_ref.shape[1:], F32)

    def ready(g):
        reads[g].wait()

    def put(d, g, o, fp, value):
        f, p = fp // 2, fp % 2
        value = value + sum_ref[d, g, o, p, f]
        if last:
            outs[d][g, o, p, f] = value.astype(BF)
        else:
            sum_ref[d, g, o, p, f] = value

    form_beams_of(offsets, chan_ref, wide_ref, order_ref, count_ref, put, ready)
    if not last:
        write = pltpu.make_async_copy(sum_ref, outs[0], sem.at[0])
        write.start()
        write.wait()


def beams_early(blocks, table, weights, order, count):
    planes, per_dest = blocks.shape[2:4]
    out = (weights.shape[1], GROUPS, planes, 2, per_dest, LOW, LANES)
    return pl.pallas_call(
        early_kernel,
        name="beams_early",
        in_specs=[VMEM] * 3 + [SMEM] * 2,
        out_specs=HBM,
        out_shape=jax.ShapeDtypeStruct(out, F32),
        scratch_shapes=[
            pltpu.VMEM((weights.shape[0], planes, 2 * per_dest, LOW, LANES), F32),
            pltpu.VMEM(out, F32),
            pltpu.VMEM(weights.shape[:2] + (3, LOW, LANES), F32),
            pltpu.SemaphoreType.DMA,
        ],
        compiler_params=params(12),
        cost_estimate=cost(8, 1 << 29),
    )(blocks, table, weights, order, count)


def beams_late(last, blocks, weights, order, count, partial):
    one = partial.shape[1:]
    members = weights.shape[0]
    if last:
        out_shape, out_specs = [jax.ShapeDtypeStruct(one, BF)] * partial.shape[0], [VMEM] * partial.shape[0]
    else:
        out_shape, out_specs = jax.ShapeDtypeStruct(partial.shape, F32), HBM
    return pl.pallas_call(
        functools.partial(late_kernel, last),
        name="beams_late",
        in_specs=[VMEM, SMEM, SMEM, HBM] + [VMEM] * len(blocks),
        out_specs=out_specs,
        out_shape=out_shape,
        scratch_shapes=[
            pltpu.VMEM(partial.shape, F32),
            pltpu.VMEM((members, partial.shape[0], 3, LOW, LANES), F32),
            pltpu.VMEM((members, one[1], one[2] * one[3], LOW, LANES), F32),
            pltpu.SemaphoreType.DMA((GROUPS,)),
        ],
        compiler_params=params(12),
        cost_estimate=cost(8, 1 << 29),
    )(weights, order, count, partial, *blocks)


def gather_kernel(me_ref, *refs):
    parts, out_ref, sem = refs[:STN], refs[STN], refs[STN + 1]
    per_dest = parts[0].shape[3]
    copies = []
    for d, part in enumerate(parts):
        frames = pl.ds((me_ref[0] ^ d) * per_dest, per_dest)
        copies.append(pltpu.make_async_copy(part, out_ref.at[:, :, :, frames], sem.at[d]))
    for copy in copies:
        copy.start()
    for copy in copies:
        copy.wait()


def gather_frames(me, parts):
    shape = parts[0].shape
    shape = shape[:3] + (shape[3] * len(parts),) + shape[4:]
    return pl.pallas_call(
        gather_kernel,
        name="gather_frames",
        in_specs=[SMEM] + [VMEM] * len(parts),
        out_specs=pl.BlockSpec(memory_space=pl.ANY),
        out_shape=jax.ShapeDtypeStruct(shape, BF),
        scratch_shapes=[pltpu.SemaphoreType.DMA((len(parts),))],
        compiler_params=params(4),
    )(me, *parts)


def swapped(value, axis, offset):
    count = lax.axis_size(axis)
    return lax.ppermute(value, axis, [(i, i ^ offset) for i in range(count)])


def fast_body(voltages, delay_table, beam_pointing, station_group):
    planes, stations_here, pols, samples_here = voltages.shape
    part, home = lax.axis_index("tf"), lax.axis_index("stn")
    me = part.astype(jnp.int32).reshape(1)
    owner = home.astype(jnp.int32).reshape(1)
    at = jnp.concatenate([me, owner])
    rows = samples_here // LANES
    volt = voltages.reshape(planes, stations_here, pols, rows, LANES)
    volt = volt.transpose(0, 1, 3, 2, 4)
    volt = volt.reshape(planes, stations_here, rows // CH_LO, CH_LO * pols, LANES)
    cosine, sine = twiddle_rows(part)
    window, first, second = window_rows(part), first_table(), second_table()

    blocks = []
    for chunk in range(CHUNKS):
        own = spread(me, volt, chunk)
        row = [own[0]]
        for d in range(1, TF):
            row.append(swapped(own[d], "tf", d))
        blocks.append(row)

    value = channel_step(at, blocks[0], window, first, cosine, sine, False)
    shape = value.shape
    value = value.reshape((STN * TF,) + shape[2:])
    value = lax.all_to_all(value, ("stn", "tf"), split_axis=0, concat_axis=0, tiled=True)
    turned = value.reshape(shape)

    own = channel_step(at, blocks[1], window, first, cosine, sine, True)
    late = [None] * STN
    for chosen, offsets in enumerate(ROUNDS):
        row = [own[chosen * TF]]
        for d in range(1, TF):
            row.append(swapped(own[chosen * TF + d], "tf", d))
        sent = middle_step(at, row, second)
        for e, value in zip(offsets, sent):
            late[e] = swapped(value, "stn", e) if e else value

    args = (delay_table, beam_pointing, station_group)
    weights = beam_weights(at, None, *args)
    partial = beams_early(turned, second, *weights)
    weights = beam_weights(at, 0, *args)
    partial = beams_late(False, late[:HALF], *weights, partial)
    weights = beam_weights(at, 1, *args)
    parts = list(beams_late(True, late[HALF:], *weights, partial))
    for d in range(1, STN):
        parts[d] = swapped(parts[d], "stn", d)
    return gather_frames(owner, parts)


def passed_along(value, axis, steps):
    count = lax.axis_size(axis)
    first, last = (max(0, -steps), min(count, count - steps))
    return lax.ppermute(value, axis, [(source, source + steps) for source in range(first, last)])


def plain_window(tap_count, points):
    position = jnp.arange(tap_count * points, dtype=jnp.int32).astype(jnp.float32)
    total_len = float(tap_count * points)
    hann_taper = 0.5 - 0.5 * jnp.cos(TWO_PI / total_len * position)
    kernel = jnp.sinc((position - 0.5 * total_len) / float(points)) * hann_taper
    return kernel.reshape(tap_count, points)


def dft_table(points):
    counter = jnp.arange(points, dtype=jnp.int32)
    product = counter[:, None] * counter[None, :] % points
    angles = TWO_PI / points * product.astype(jnp.float32)
    factor = 1.0 / math.sqrt(points)
    cosine = jnp.cos(angles) * factor
    sine_part = jnp.sin(angles) * factor
    stacked = jnp.stack([jnp.stack([cosine, sine_part]), jnp.stack([-sine_part, cosine])])
    return stacked.astype(jnp.bfloat16)


def channelize(extended, frame_count):
    points = CH_LO * CH_HI
    window = plain_window(TAPS, points)
    filtered = sum(
        (
            window[tap_step]
            * extended[:, :, :, tap_step : tap_step + frame_count, :].astype(jnp.float32)
            for tap_step in range(TAPS)
        )
    )
    filtered = filtered.astype(jnp.bfloat16)
    shaped = filtered.reshape(filtered.shape[:4] + (CH_LO, CH_HI))
    section_one = jnp.einsum(
        "oikn,ispfnm->ospfkm", dft_table(CH_LO), shaped, preferred_element_type=jnp.float32
    )
    low_index = jnp.arange(CH_LO, dtype=jnp.int32)
    high_index = jnp.arange(CH_HI, dtype=jnp.int32)
    twiddle = TWO_PI / points * (low_index[:, None] * high_index[None, :]).astype(jnp.float32)
    cosine = jnp.cos(twiddle)
    sine_part = jnp.sin(twiddle)
    rotated = jnp.stack(
        [
            section_one[0] * cosine + section_one[1] * sine_part,
            section_one[1] * cosine - section_one[0] * sine_part,
        ]
    ).astype(jnp.bfloat16)
    return jnp.einsum(
        "oimj,ispfkm->ospfkj", dft_table(CH_HI), rotated, preferred_element_type=jnp.float32
    ).astype(jnp.bfloat16)


def plain_weights(delays, beam_ids, groups, channel_low, station_total):
    points = CH_LO * CH_HI
    member = (groups[None, :] == (beam_ids % GROUPS)[:, None]).astype(jnp.float32)
    weight_scale = math.sqrt(GROUPS / station_total) * member
    channel = channel_low[:, None] + CH_LO * jnp.arange(CH_HI, dtype=jnp.int32)[None, :]
    fraction = channel.astype(jnp.float32) / float(points)
    phases = TWO_PI * (delays[:, :, None, None] * fraction[None, None])
    weight_re = (weight_scale[:, :, None, None] * jnp.cos(phases)).astype(jnp.bfloat16)
    weight_im = (-weight_scale[:, :, None, None] * jnp.sin(phases)).astype(jnp.bfloat16)
    return (weight_re, weight_im)


def form_beams(weight_re, weight_im, channels):
    real_in = channels[0]
    imag_in = channels[1]

    def contract(weights_part, data_part):
        return jnp.einsum(
            "bsxc,spfxc->bpfxc", weights_part, data_part, preferred_element_type=jnp.float32
        )

    real_out = contract(weight_re, real_in) - contract(weight_im, imag_in)
    imag_out = contract(weight_re, imag_in) + contract(weight_im, real_in)
    return jnp.stack([real_out, imag_out], axis=1)


def select_delays(delay_rows, pointing):
    directions = jnp.arange(delay_rows.shape[0], dtype=jnp.int32)
    onehot = (pointing[:, None] == directions[None, :]).astype(jnp.float32)
    return jnp.dot(
        onehot, delay_rows, precision=lax.Precision.HIGHEST, preferred_element_type=jnp.float32
    )


def with_history(frames_own):
    frame_count = frames_own.shape[3]
    needed = TAPS - 1
    pieces = []
    hop_count = (needed + frame_count - 1) // frame_count
    for hop_step in range(1, hop_count + 1):
        take_count = min(frame_count, needed - (hop_step - 1) * frame_count)
        portion = frames_own[:, :, :, frame_count - take_count :, :]
        pieces.append(passed_along(portion, "tf", hop_step))
    return jnp.concatenate(pieces[::-1] + [frames_own], axis=3)


def plain_body(voltages, delay_table, beam_pointing, station_group):
    planes, stations_here, pol_count, samples_here = voltages.shape
    points = CH_LO * CH_HI
    frame_count = samples_here // points
    frames_own = voltages.reshape(planes, stations_here, pol_count, frame_count, points)
    channels = channelize(with_history(frames_own), frame_count)
    station_total = station_group.shape[0]
    beam_total = beam_pointing.shape[0]
    regrouped = lax.all_to_all(channels, "stn", split_axis=4, concat_axis=1, tiled=True)
    low_count = regrouped.shape[4]
    channel_low = lax.axis_index("stn") * low_count + jnp.arange(low_count, dtype=jnp.int32)
    beam_ids = jnp.arange(beam_total, dtype=jnp.int32)
    delays_all = select_delays(delay_table, beam_pointing)
    weight_re, weight_im = plain_weights(
        delays_all, beam_ids, station_group, channel_low, station_total
    )
    formed = form_beams(weight_re, weight_im, regrouped).astype(jnp.bfloat16)
    result = lax.all_to_all(
        lax.all_to_all(formed, "stn", split_axis=0, concat_axis=4, tiled=True),
        "tf",
        split_axis=4,
        concat_axis=3,
        tiled=True,
    )
    return result


def solution(mesh):
    in_specs = (P(None, "stn", None, "tf"), P(), P(), P())
    out_specs = P("stn", None, None, None, "tf", None)

    def spread_over(body):
        return jax.shard_map(
            body, mesh=mesh, in_specs=in_specs, out_specs=out_specs, check_vma=False
        )

    if mesh.shape["tf"] == TF and mesh.shape["stn"] == STN:
        return spread_over(fast_body)
    return spread_over(plain_body)
```

```python
import functools
import math

import jax
import jax.numpy as jnp
import numpy as np
from jax import lax
from jax.experimental import pallas as pl
from jax.experimental.pallas import tpu as pltpu
from jax.sharding import PartitionSpec as P


TAPS = 16
CH_LO = 32
CH_HI = 128
GROUPS = 4
POINTS = CH_LO * CH_HI
TWO_PI = 2.0 * math.pi
BF = jnp.bfloat16
F32 = jnp.float32

LANES = 128
TF = 4
STN = 8
HALF = STN // 2
UNROLL = 8
TURNS = ((4, 2, 5, 6), (3, 7, 1, 0))
ROUNDS = ((2, 3, 4, 5), (0, 1, 6, 7))


def offset_in(chosen, place):
    return place + 4 * (place // 2) if chosen else place + 2


PART = CH_HI // TF
LOW = CH_LO // TF
PER = 4
CHUNKS = 2


def filter_window(position):
    total_len = float(TAPS * POINTS)
    value = position.astype(F32)
    hann_taper = 0.5 - 0.5 * jnp.cos(TWO_PI / total_len * value)
    return jnp.sinc((value - 0.5 * total_len) / float(POINTS)) * hann_taper


def window_rows(part):
    shape = (TAPS, 2 * CH_LO, LANES)
    tap = lax.broadcasted_iota(jnp.int32, shape, 0)
    n2 = lax.broadcasted_iota(jnp.int32, shape, 1) // 2
    n1 = part * PART + lax.broadcasted_iota(jnp.int32, shape, 2) % PART
    return filter_window(tap * POINTS + n2 * CH_HI + n1)


def dft_pair(points):
    counter = np.arange(points)
    angles = TWO_PI / points * (counter[:, None] * counter[None, :] % points)
    factor = 1.0 / math.sqrt(points)
    return np.cos(angles) * factor, np.sin(angles) * factor


def first_table():
    cosine, sine = dft_pair(CH_LO)
    planes = np.stack([np.stack([cosine, sine]), np.stack([-sine, cosine])])
    planes = planes.reshape(2, 2, TF, LOW, CH_LO)
    table = np.einsum("oitkn,pr->otpkinr", planes, np.eye(2))
    return jnp.asarray(table.reshape(2, TF, 2 * LOW, 4 * CH_LO), BF)


def second_table():
    cosine, sine = dft_pair(CH_HI)
    table = np.block([[cosine, -sine], [sine, cosine]])
    return jnp.asarray(table.reshape(2, TF, PART, 2 * CH_HI), BF)


def twiddle_rows(part):
    shape = (TF, 2 * LOW, LANES)
    k2 = lax.broadcasted_iota(jnp.int32, shape, 0) * LOW
    k2 = k2 + lax.broadcasted_iota(jnp.int32, shape, 1) % LOW
    n1 = part * PART + lax.broadcasted_iota(jnp.int32, shape, 2) % PART
    angle = TWO_PI / POINTS * (k2 * n1).astype(F32)
    return jnp.cos(angle), jnp.sin(angle)


VMEM = pl.BlockSpec(memory_space=pltpu.VMEM)
SMEM = pl.BlockSpec(memory_space=pltpu.SMEM)
HBM = pl.BlockSpec(memory_space=pltpu.HBM)


def params(mib):
    return pltpu.CompilerParams(vmem_limit_bytes=mib << 20)


def cost(mib, flops=0):
    return pl.CostEstimate(flops=flops, bytes_accessed=mib << 20, transcendentals=0)


def swap_lane_blocks(parts):
    lane = lax.broadcasted_iota(jnp.int32, parts[0].shape, 1)
    upper = lane >= 2 * PART
    odd = (lane // PART) % 2 == 1
    turned = [pltpu.roll(part, 2 * PART, 1) for part in parts]
    half = [
        jnp.where(upper, turned[2], parts[0]),
        jnp.where(upper, turned[3], parts[1]),
        jnp.where(upper, parts[2], turned[0]),
        jnp.where(upper, parts[3], turned[1]),
    ]
    out = []
    for low, high in ((half[0], half[1]), (half[2], half[3])):
        out.append(jnp.where(odd, pltpu.roll(high, PART, 1), low))
        out.append(jnp.where(odd, high, pltpu.roll(low, LANES - PART, 1)))
    return out


def spread_kernel(chunk, me_ref, volt_ref, *refs):
    outs, (in_ref, sem) = refs[:TF], refs[TF:]
    planes, _, frames = volt_ref.shape[:3]
    half = frames // 2
    steps = [(q, part) for q in range(planes) for part in range(2)]
    reads = [
        pltpu.make_async_copy(
            volt_ref.at[q, pl.ds(chunk * PER, PER), pl.ds(part * half, half)],
            in_ref.at[q, :, pl.ds(part * half, half)],
            sem.at[q, part],
        )
        for q, part in steps
    ]
    for read in reads:
        read.start()
    for (q, part), read in zip(steps, reads):
        read.wait()
        for me in range(TF):

            @pl.when(me_ref[0] == me)
            def _(me=me, q=q, part=part):
                def one(f, carry):
                    parts = [in_ref[q, a, f] for a in range(PER)]
                    for j, block in enumerate(swap_lane_blocks(parts)):
                        outs[j ^ me][q, f] = block
                    return carry

                lax.fori_loop(part * half, (part + 1) * half, one, 0, unroll=2)


def spread(me, volt, chunk):
    planes, _, frames, rows, _ = volt.shape
    return pl.pallas_call(
        functools.partial(spread_kernel, chunk),
        name="spread",
        in_specs=[SMEM, HBM],
        out_specs=[VMEM] * TF,
        out_shape=[jax.ShapeDtypeStruct((planes, frames, rows, LANES), BF)] * TF,
        scratch_shapes=[
            pltpu.VMEM((planes, PER, frames, rows, LANES), BF),
            pltpu.SemaphoreType.DMA((planes, 2)),
        ],
        compiler_params=params(4),
        cost_estimate=cost(4),
    )(me, pltpu.with_memory_space_constraint(volt, pltpu.HBM))


def channel_kernel(split, at_ref, *refs):
    sources = refs[:TF]
    win_ref, table_ref, cos_ref, sin_ref = refs[TF : TF + 4]
    stage_ref, filt_ref = refs[-2:] if split else refs[-4:-2]
    me, owner = at_ref[0], at_ref[1]
    rows = 2 * CH_LO
    history = TAPS - 1
    planes, per_source = sources[0].shape[:2]
    frames = TF * per_source
    for d, ref in enumerate(sources):
        stage_ref[:, pl.ds((me ^ d) * per_source, per_source)] = ref[...]

    strip = 16

    def one_strip(q, step, carry):
        at = pl.multiple_of(step * strip, strip)
        data = [stage_ref[q, f, pl.ds(at, strip), :].astype(F32) for f in range(frames)]
        taps = [win_ref[tap, pl.ds(at, strip), :] for tap in range(TAPS)]
        for f in range(frames):
            total = None
            for tap in range(max(0, history - f), TAPS):
                term = taps[tap] * data[f + tap - history]
                total = term if total is None else total + term
            filt_ref[f, q, pl.ds(at, strip), :] = total.astype(BF)
        return carry

    for q in range(planes):
        lax.fori_loop(0, rows // strip, functools.partial(one_strip, q), 0)

    ranges = [(me ^ t) if split else t for t in range(TF)]
    table = jnp.concatenate([table_ref[o, t] for o in range(planes) for t in ranges], axis=0)
    per_dest = frames // STN
    if split:
        outs = refs[TF + 4 : TF + 4 + 2 * TF]
    else:
        out_ref, done_ref, sem = refs[TF + 4], refs[-2], refs[-1]

        def send(dest):
            return pltpu.make_async_copy(done_ref.at[dest], out_ref.at[dest], sem.at[dest])

    def one_dest(chosen, step, carry):
        dest = owner ^ offset_in(chosen, step) if split else step
        cosine = jnp.concatenate([cos_ref[t] for t in ranges], axis=0)
        sine = jnp.concatenate([sin_ref[t] for t in ranges], axis=0)
        for pair in range(per_dest // 2):
            f = per_dest * dest + 2 * pair
            left = filt_ref[f].reshape(2 * rows, LANES)
            right = filt_ref[f + 1].reshape(2 * rows, LANES)
            both = jnp.concatenate([left, right], axis=1)
            spectrum = jnp.dot(table, both, preferred_element_type=F32)
            for side in range(2):
                real = spectrum[:rows, side * LANES : (side + 1) * LANES]
                imag = spectrum[rows:, side * LANES : (side + 1) * LANES]
                turned = (real * cosine + imag * sine, imag * cosine - real * sine)
                for o in range(2):
                    value = turned[o].astype(BF).reshape(TF, 2 * LOW, LANES)
                    if split:
                        for d in range(TF):
                            outs[chosen * TF + d][step, o, 2 * pair + side] = value[d]
                    else:
                        done_ref[dest, :, o, 2 * pair + side] = value
        if not split:
            send(dest).start()
        return carry

    if split:
        for chosen in range(2):
            lax.fori_loop(0, HALF, functools.partial(one_dest, chosen), 0, unroll=2)
    else:
        lax.fori_loop(0, STN, functools.partial(one_dest, 0), 0, unroll=2)
        for dest in range(STN):
            send(dest).wait()


def channel_step(at, blocks, window, table, cosine, sine, split):
    planes, per_source, rows, _ = blocks[0].shape
    frames = TF * per_source
    tail = (planes, frames // STN, 2 * LOW, LANES)
    scratch = [
        pltpu.VMEM((planes, frames, rows, LANES), BF),
        pltpu.VMEM((frames, planes, rows, LANES), BF),
    ]
    if split:
        out_shape = [jax.ShapeDtypeStruct((HALF,) + tail, BF)] * (2 * TF)
        out_specs = [VMEM] * (2 * TF)
    else:
        out = (STN, TF) + tail
        out_shape, out_specs = jax.ShapeDtypeStruct(out, BF), HBM
        scratch += [pltpu.VMEM(out, BF), pltpu.SemaphoreType.DMA((STN,))]
    return pl.pallas_call(
        functools.partial(channel_kernel, split),
        name="channel_step",
        in_specs=[SMEM] + [VMEM] * (TF + 4),
        out_specs=out_specs,
        out_shape=out_shape,
        scratch_shapes=scratch,
        compiler_params=params(12),
        cost_estimate=cost(8, 1 << 29),
    )(at, *blocks, window, table, cosine, sine)


def turned_by(turns):
    quarter = jnp.round(4.0 * turns)
    angle = TWO_PI * (turns - 0.25 * quarter)
    square = angle * angle
    sine = angle * (
        1.0 + square * (-1.0 / 6 + square * (1.0 / 120 + square * (-1.0 / 5040 + square * (1.0 / 362880))))
    )
    cosine = 1.0 + square * (
        -0.5 + square * (1.0 / 24 + square * (-1.0 / 720 + square * (1.0 / 40320)))
    )
    turn = quarter.astype(jnp.int32) & 3
    odd = (turn & 1) == 1
    base_cos = jnp.where(odd, sine, cosine)
    base_sin = jnp.where(odd, cosine, sine)
    real = jnp.where((turn == 1) | (turn == 2), -base_cos, base_cos)
    return real, jnp.where(turn >= 2, -base_sin, base_sin)


def weight_kernel(chunk, offset_of, at_ref, table_ref, beam_ref, group_ref, out_ref, order_ref, count_ref, row_ref):
    total = group_ref.shape[0]
    members = out_ref.shape[0] - 1
    offsets = out_ref.shape[1]
    scale = math.sqrt(GROUPS / total)
    shape = (LOW, LANES)
    sublane = lax.broadcasted_iota(jnp.int32, shape, 0)
    lane = lax.broadcasted_iota(jnp.int32, shape, 1)
    high = (at_ref[0] * LOW + CH_LO * lane).astype(F32) / float(POINTS)
    low = sublane.astype(F32) / float(POINTS)
    for g in range(GROUPS):
        count_ref[g] = 0

    def some_members(step, carry):
        for slot in range(UNROLL):
            one_member(step * UNROLL + slot, slot)
        return carry

    def one_member(member, slot):
        source = offset_of(member // PER, at_ref[1])
        s = source * (PER * CHUNKS) + chunk * PER + member % PER
        group = group_ref[s]
        at = count_ref[group]
        order_ref[group, at] = member
        order_ref[group, at + 1] = members
        count_ref[group] = at + 1

        down = jnp.zeros(shape, F32)
        across = jnp.zeros(shape, F32)
        for d in range(offsets):
            beam = group + GROUPS * (at_ref[1] ^ d)
            delay = table_ref[beam_ref[beam], s]
            down = jnp.where(sublane == d, delay, down)
            across = jnp.where(lane == d, delay, across)
        real, imag = turned_by(down * high)
        row_ref[slot, 0] = scale * real
        row_ref[slot, 1] = -scale * imag
        real, imag = turned_by(across * low)
        imag = -imag
        for d in range(offsets):
            high_re = row_ref[slot, 0, pl.ds(d, 1), :]
            high_im = row_ref[slot, 1, pl.ds(d, 1), :]
            low_re = jnp.broadcast_to(real[:, d : d + 1], shape)
            low_im = jnp.broadcast_to(imag[:, d : d + 1], shape)
            out_ref[member, d, 0] = (high_re * low_re - high_im * low_im).astype(BF)
            out_ref[member, d, 1] = (high_re * low_im + high_im * low_re).astype(BF)

    out_ref[members] = jnp.zeros(out_ref.shape[1:], BF)
    lax.fori_loop(0, members // UNROLL, some_members, 0)


def beam_weights(at, chosen, delay_table, beam_pointing, station_group):
    chunk = 0 if chosen is None else 1
    members = (HALF if chunk else STN) * PER

    def offset_of(place, owner):
        return place if chosen is None else (chosen * HALF + place) ^ owner

    offsets = beam_pointing.shape[0] // GROUPS
    out = (members + 1, offsets, 2, LOW, LANES)
    return pl.pallas_call(
        functools.partial(weight_kernel, chunk, offset_of),
        name="beam_weights",
        in_specs=[SMEM] * 4,
        out_specs=[VMEM, SMEM, SMEM],
        out_shape=[
            jax.ShapeDtypeStruct(out, BF),
            jax.ShapeDtypeStruct((GROUPS, members + 2), jnp.int32),
            jax.ShapeDtypeStruct((GROUPS,), jnp.int32),
        ],
        scratch_shapes=[pltpu.VMEM((UNROLL, 2, LOW, LANES), F32)],
        compiler_params=params(8),
        cost_estimate=cost(8, 1 << 29),
    )(at, delay_table, beam_pointing, station_group)


def transform(parts_of, table, put):
    planes = [swap_lane_blocks(parts_of(o)) for o in range(2)]
    for a in range(PER):
        both = jnp.concatenate([planes[0][a], planes[1][a]], axis=1)
        spectrum = jnp.dot(both, table, preferred_element_type=F32)
        for o in range(2):
            put(a, o, spectrum[:, o * LANES : (o + 1) * LANES])


def table_of(table_ref, parts):
    return jnp.concatenate([table_ref[q, j] for q in range(2) for j in parts], axis=0)


def middle_kernel(at_ref, *refs):
    blocks, table_ref, outs = refs[:TF], refs[TF], refs[TF + 1 :]
    me = at_ref[0]
    per_dest = blocks[0].shape[2]
    table = table_of(table_ref, [me ^ d for d in range(TF)])
    for place, out in enumerate(outs):

        def parts_of(o, place=place):
            return [block[place, o].reshape(per_dest * 2 * LOW, LANES) for block in blocks]

        def put(a, o, value, out=out):
            out[a, o] = value.astype(BF)

        transform(parts_of, table, put)


def middle_step(at, blocks, table):
    _, planes, per_dest, _, _ = blocks[0].shape
    out = (PER, planes, per_dest * 2 * LOW, LANES)
    return pl.pallas_call(
        middle_kernel,
        name="middle_step",
        in_specs=[SMEM] + [VMEM] * (TF + 1),
        out_specs=[VMEM] * HALF,
        out_shape=[jax.ShapeDtypeStruct(out, BF)] * HALF,
        compiler_params=params(4),
        cost_estimate=cost(4, 1 << 28),
    )(at, *blocks, table)


def spread_weights(offsets, weight_ref, wide_ref):
    def one(member, carry):
        for i, d in enumerate(offsets):
            real, imag = weight_ref[member, d, 0].astype(F32), weight_ref[member, d, 1].astype(F32)
            wide_ref[member, i, 0] = real
            wide_ref[member, i, 1] = imag - real
            wide_ref[member, i, 2] = imag + real
        return carry

    last = weight_ref.shape[0] - 1
    lax.fori_loop(0, last, one, 0, unroll=4)
    one(last, 0)


def form_beams_of(offsets, chan_ref, wide_ref, order_ref, count_ref, put, ready=lambda g: None, done=lambda g: None):
    count = len(offsets)
    wide = 16 // count
    blocks = chan_ref.shape[2] // wide

    def one_block(g, step, carry):
        base = step * wide

        def one_pair(pair, acc):
            acc = list(acc)
            for member in (order_ref[g, 2 * pair], order_ref[g, 2 * pair + 1]):
                data = []
                for x in range(wide):
                    re, im = chan_ref[member, 0, base + x], chan_ref[member, 1, base + x]
                    data.append((re + im, re, im))
                for i, d in enumerate(offsets):
                    for y in range(3):
                        weight = wide_ref[member, i, y]
                        for x in range(wide):
                            at = (i * 3 + y) * wide + x
                            acc[at] = acc[at] + weight * data[x][y]
            return tuple(acc)

        zero = jnp.zeros((LOW, LANES), F32)
        pairs = (count_ref[g] + 1) // 2
        acc = lax.fori_loop(0, pairs, one_pair, (zero,) * (3 * count * wide))
        for i, d in enumerate(offsets):
            for x in range(wide):
                both, re, im = (acc[(i * 3 + y) * wide + x] for y in range(3))
                put(d, g, 0, base + x, both - im)
                put(d, g, 1, base + x, both + re)
        return carry

    for g in range(GROUPS):
        ready(g)
        lax.fori_loop(0, blocks, functools.partial(one_block, g), 0)
        done(g)


def group_copies(source, target, sem):
    return [pltpu.make_async_copy(source.at[:, g], target.at[:, g], sem.at[g]) for g in range(GROUPS)]


def early_kernel(blocks_ref, table_ref, weight_ref, order_ref, count_ref, sum_hbm, chan_ref, sum_ref, wide_ref, sem):
    offsets = range(weight_ref.shape[1])
    spread_weights(offsets, weight_ref, wide_ref)
    sources, _, _, per_dest = blocks_ref.shape[:4]
    table = table_of(table_ref, range(TF))
    for src in range(sources):

        def parts_of(o, src=src):
            return [blocks_ref[src, j, o].reshape(per_dest * 2 * LOW, LANES) for j in range(TF)]

        def put(a, o, value, src=src):
            chan_ref[src * PER + a, o] = value.reshape(per_dest * 2, LOW, LANES)

        transform(parts_of, table, put)
    chan_ref[chan_ref.shape[0] - 1] = jnp.zeros(chan_ref.shape[1:], F32)


    def keep(d, g, o, fp, value):
        sum_ref[d, g, o, fp % 2, fp // 2] = value

    writes = group_copies(sum_ref, sum_hbm, sem)
    form_beams_of(
        offsets, chan_ref, wide_ref, order_ref, count_ref, keep, done=lambda g: writes[g].start()
    )
    for write in writes:
        write.wait()


def late_kernel(last, offsets, weight_ref, order_ref, count_ref, sum_hbm, *refs):
    sum_ref, wide_ref, chan_ref, sem = refs[-4:]
    sources = chan_ref.shape[0] // PER
    blocks, outs = refs[:sources], refs[sources:-4]
    reads = group_copies(sum_hbm, sum_ref, sem)
    for read in reads:
        read.start()
    spread_weights(offsets, weight_ref, wide_ref)
    members, planes, both = chan_ref.shape[:3]
    for place, block in enumerate(blocks):
        value = block[...].astype(F32)
        chan_ref[pl.ds(place * PER, PER)] = value.reshape(PER, planes, both, LOW, LANES)
    chan_ref[members - 1] = jnp.zeros(chan_ref.shape[1:], F32)

    def ready(g):
        reads[g].wait()

    def put(d, g, o, fp, value):
        f, p = fp // 2, fp % 2
        value = value + sum_ref[d, g, o, p, f]
        if last:
            outs[offsets.index(d)][g, o, p, f] = value.astype(BF)
        else:
            sum_ref[d, g, o, p, f] = value

    writes = [] if last else group_copies(sum_ref, outs[0], sem)

    def done(g):
        if not last:
            writes[g].start()

    form_beams_of(offsets, chan_ref, wide_ref, order_ref, count_ref, put, ready, done)
    for write in writes:
        write.wait()


def beams_early(blocks, table, weights, order, count):
    planes, per_dest = blocks.shape[2:4]
    out = (weights.shape[1], GROUPS, planes, 2, per_dest, LOW, LANES)
    return pl.pallas_call(
        early_kernel,
        name="beams_early",
        in_specs=[VMEM] * 3 + [SMEM] * 2,
        out_specs=HBM,
        out_shape=jax.ShapeDtypeStruct(out, F32),
        scratch_shapes=[
            pltpu.VMEM((weights.shape[0], planes, 2 * per_dest, LOW, LANES), F32),
            pltpu.VMEM(out, F32),
            pltpu.VMEM(weights.shape[:2] + (3, LOW, LANES), F32),
            pltpu.SemaphoreType.DMA((GROUPS,)),
        ],
        compiler_params=params(12),
        cost_estimate=cost(8, 1 << 29),
    )(blocks, table, weights, order, count)


def beams_late(last, offsets, blocks, weights, order, count, partial):
    one = partial.shape[1:]
    members = weights.shape[0]
    if last:
        out_shape, out_specs = [jax.ShapeDtypeStruct(one, BF)] * len(offsets), [VMEM] * len(offsets)
    else:
        out_shape, out_specs = jax.ShapeDtypeStruct(partial.shape, F32), HBM
    return pl.pallas_call(
        functools.partial(late_kernel, last, offsets),
        name="beams_late",
        in_specs=[VMEM, SMEM, SMEM, HBM] + [VMEM] * len(blocks),
        out_specs=out_specs,
        out_shape=out_shape,
        scratch_shapes=[
            pltpu.VMEM(partial.shape, F32),
            pltpu.VMEM((members, len(offsets), 3, LOW, LANES), F32),
            pltpu.VMEM((members, one[1], one[2] * one[3], LOW, LANES), F32),
            pltpu.SemaphoreType.DMA((GROUPS,)),
        ],
        compiler_params=params(12),
        cost_estimate=cost(8, 1 << 29),
    )(weights, order, count, partial, *blocks)


def gather_kernel(me_ref, *refs):
    parts, out_ref, sem = refs[:STN], refs[STN], refs[STN + 1]
    per_dest = parts[0].shape[3]
    copies = []
    for d, part in enumerate(parts):
        frames = pl.ds((me_ref[0] ^ d) * per_dest, per_dest)
        copies.append(pltpu.make_async_copy(part, out_ref.at[:, :, :, frames], sem.at[d]))
    for copy in copies:
        copy.start()
    for copy in copies:
        copy.wait()


def gather_frames(me, parts):
    shape = parts[0].shape
    shape = shape[:3] + (shape[3] * len(parts),) + shape[4:]
    return pl.pallas_call(
        gather_kernel,
        name="gather_frames",
        in_specs=[SMEM] + [VMEM] * len(parts),
        out_specs=pl.BlockSpec(memory_space=pl.ANY),
        out_shape=jax.ShapeDtypeStruct(shape, BF),
        scratch_shapes=[pltpu.SemaphoreType.DMA((len(parts),))],
        compiler_params=params(4),
    )(me, *parts)


def swapped(value, axis, offset):
    count = lax.axis_size(axis)
    return lax.ppermute(value, axis, [(i, i ^ offset) for i in range(count)])


def fast_body(voltages, delay_table, beam_pointing, station_group):
    planes, stations_here, pols, samples_here = voltages.shape
    part, home = lax.axis_index("tf"), lax.axis_index("stn")
    me = part.astype(jnp.int32).reshape(1)
    owner = home.astype(jnp.int32).reshape(1)
    at = jnp.concatenate([me, owner])
    rows = samples_here // LANES
    volt = voltages.reshape(planes, stations_here, pols, rows, LANES)
    volt = volt.transpose(0, 1, 3, 2, 4)
    volt = volt.reshape(planes, stations_here, rows // CH_LO, CH_LO * pols, LANES)
    cosine, sine = twiddle_rows(part)
    window, first, second = window_rows(part), first_table(), second_table()

    blocks = []
    for chunk in range(CHUNKS):
        own = spread(me, volt, chunk)
        row = [own[0]]
        for d in range(1, TF):
            row.append(swapped(own[d], "tf", d))
        blocks.append(row)

    value = channel_step(at, blocks[0], window, first, cosine, sine, False)
    shape = value.shape
    value = value.reshape((STN * TF,) + shape[2:])
    value = lax.all_to_all(value, ("stn", "tf"), split_axis=0, concat_axis=0, tiled=True)
    turned = value.reshape(shape)

    own = channel_step(at, blocks[1], window, first, cosine, sine, True)
    late = [None] * STN
    for chosen, offsets in enumerate(ROUNDS):
        row = [own[chosen * TF]]
        for d in range(1, TF):
            row.append(swapped(own[chosen * TF + d], "tf", d))
        sent = middle_step(at, row, second)
        for e, value in zip(offsets, sent):
            late[e] = swapped(value, "stn", e) if e else value

    args = (delay_table, beam_pointing, station_group)
    weights = beam_weights(at, None, *args)
    partial = beams_early(turned, second, *weights)
    weights = beam_weights(at, 0, *args)
    partial = beams_late(False, range(STN), late[:HALF], *weights, partial)
    weights = beam_weights(at, 1, *args)
    parts = [None] * STN
    for offsets in TURNS:
        made = beams_late(True, offsets, late[HALF:], *weights, partial)
        for d, value in zip(offsets, made):
            parts[d] = swapped(value, "stn", d) if d else value
    return gather_frames(owner, parts)


def passed_along(value, axis, steps):
    count = lax.axis_size(axis)
    first, last = (max(0, -steps), min(count, count - steps))
    return lax.ppermute(value, axis, [(source, source + steps) for source in range(first, last)])


def plain_window(tap_count, points):
    position = jnp.arange(tap_count * points, dtype=jnp.int32).astype(jnp.float32)
    total_len = float(tap_count * points)
    hann_taper = 0.5 - 0.5 * jnp.cos(TWO_PI / total_len * position)
    kernel = jnp.sinc((position - 0.5 * total_len) / float(points)) * hann_taper
    return kernel.reshape(tap_count, points)


def dft_table(points):
    counter = jnp.arange(points, dtype=jnp.int32)
    product = counter[:, None] * counter[None, :] % points
    angles = TWO_PI / points * product.astype(jnp.float32)
    factor = 1.0 / math.sqrt(points)
    cosine = jnp.cos(angles) * factor
    sine_part = jnp.sin(angles) * factor
    stacked = jnp.stack([jnp.stack([cosine, sine_part]), jnp.stack([-sine_part, cosine])])
    return stacked.astype(jnp.bfloat16)


def channelize(extended, frame_count):
    points = CH_LO * CH_HI
    window = plain_window(TAPS, points)
    filtered = sum(
        (
            window[tap_step]
            * extended[:, :, :, tap_step : tap_step + frame_count, :].astype(jnp.float32)
            for tap_step in range(TAPS)
        )
    )
    filtered = filtered.astype(jnp.bfloat16)
    shaped = filtered.reshape(filtered.shape[:4] + (CH_LO, CH_HI))
    section_one = jnp.einsum(
        "oikn,ispfnm->ospfkm", dft_table(CH_LO), shaped, preferred_element_type=jnp.float32
    )
    low_index = jnp.arange(CH_LO, dtype=jnp.int32)
    high_index = jnp.arange(CH_HI, dtype=jnp.int32)
    twiddle = TWO_PI / points * (low_index[:, None] * high_index[None, :]).astype(jnp.float32)
    cosine = jnp.cos(twiddle)
    sine_part = jnp.sin(twiddle)
    rotated = jnp.stack(
        [
            section_one[0] * cosine + section_one[1] * sine_part,
            section_one[1] * cosine - section_one[0] * sine_part,
        ]
    ).astype(jnp.bfloat16)
    return jnp.einsum(
        "oimj,ispfkm->ospfkj", dft_table(CH_HI), rotated, preferred_element_type=jnp.float32
    ).astype(jnp.bfloat16)


def plain_weights(delays, beam_ids, groups, channel_low, station_total):
    points = CH_LO * CH_HI
    member = (groups[None, :] == (beam_ids % GROUPS)[:, None]).astype(jnp.float32)
    weight_scale = math.sqrt(GROUPS / station_total) * member
    channel = channel_low[:, None] + CH_LO * jnp.arange(CH_HI, dtype=jnp.int32)[None, :]
    fraction = channel.astype(jnp.float32) / float(points)
    phases = TWO_PI * (delays[:, :, None, None] * fraction[None, None])
    weight_re = (weight_scale[:, :, None, None] * jnp.cos(phases)).astype(jnp.bfloat16)
    weight_im = (-weight_scale[:, :, None, None] * jnp.sin(phases)).astype(jnp.bfloat16)
    return (weight_re, weight_im)


def form_beams(weight_re, weight_im, channels):
    real_in = channels[0]
    imag_in = channels[1]

    def contract(weights_part, data_part):
        return jnp.einsum(
            "bsxc,spfxc->bpfxc", weights_part, data_part, preferred_element_type=jnp.float32
        )

    real_out = contract(weight_re, real_in) - contract(weight_im, imag_in)
    imag_out = contract(weight_re, imag_in) + contract(weight_im, real_in)
    return jnp.stack([real_out, imag_out], axis=1)


def select_delays(delay_rows, pointing):
    directions = jnp.arange(delay_rows.shape[0], dtype=jnp.int32)
    onehot = (pointing[:, None] == directions[None, :]).astype(jnp.float32)
    return jnp.dot(
        onehot, delay_rows, precision=lax.Precision.HIGHEST, preferred_element_type=jnp.float32
    )


def with_history(frames_own):
    frame_count = frames_own.shape[3]
    needed = TAPS - 1
    pieces = []
    hop_count = (needed + frame_count - 1) // frame_count
    for hop_step in range(1, hop_count + 1):
        take_count = min(frame_count, needed - (hop_step - 1) * frame_count)
        portion = frames_own[:, :, :, frame_count - take_count :, :]
        pieces.append(passed_along(portion, "tf", hop_step))
    return jnp.concatenate(pieces[::-1] + [frames_own], axis=3)


def plain_body(voltages, delay_table, beam_pointing, station_group):
    planes, stations_here, pol_count, samples_here = voltages.shape
    points = CH_LO * CH_HI
    frame_count = samples_here // points
    frames_own = voltages.reshape(planes, stations_here, pol_count, frame_count, points)
    channels = channelize(with_history(frames_own), frame_count)
    station_total = station_group.shape[0]
    beam_total = beam_pointing.shape[0]
    regrouped = lax.all_to_all(channels, "stn", split_axis=4, concat_axis=1, tiled=True)
    low_count = regrouped.shape[4]
    channel_low = lax.axis_index("stn") * low_count + jnp.arange(low_count, dtype=jnp.int32)
    beam_ids = jnp.arange(beam_total, dtype=jnp.int32)
    delays_all = select_delays(delay_table, beam_pointing)
    weight_re, weight_im = plain_weights(
        delays_all, beam_ids, station_group, channel_low, station_total
    )
    formed = form_beams(weight_re, weight_im, regrouped).astype(jnp.bfloat16)
    result = lax.all_to_all(
        lax.all_to_all(formed, "stn", split_axis=0, concat_axis=4, tiled=True),
        "tf",
        split_axis=4,
        concat_axis=3,
        tiled=True,
    )
    return result


def solution(mesh):
    in_specs = (P(None, "stn", None, "tf"), P(), P(), P())
    out_specs = P("stn", None, None, None, "tf", None)

    def spread_over(body):
        return jax.shard_map(
            body, mesh=mesh, in_specs=in_specs, out_specs=out_specs, check_vma=False
        )

    if mesh.shape["tf"] == TF and mesh.shape["stn"] == STN:
        return spread_over(fast_body)
    return spread_over(plain_body)
```
